768 devices in a mesh: fluid: 2 (over core), zon: 96 (over x, z, y_lo), mer: 4 (over y_hi).
Axes of the slice: x: 4, y: 8 (y_hi: 4, y_lo: 2; y = y_hi * 2 + y_lo), z: 12, core: 2. Of those that a mesh axis runs over, the one named last changes fastest.
Arguments:
- state: float32 [2, 2, 64, 1536, 512], P('fluid', None, None, 'zon', 'mer'), may hold values from -6 to 6
- flow: bfloat16 [2, 2, 64, 1536, 512], P('fluid', None, None, 'zon', 'mer'), may hold values from -0.5 to 0.5
- diffusion: float32 [2, 2, 64], P('fluid'), may hold values from 0.02 to 0.2
- column_solve: float32 [2, 64, 64], P('fluid'), may hold values from -1 to 1, as said below
- exchange_rate: float32 [2, 2], P('fluid'), may hold values from 0.2 to 0.6
- block_map: int32 [16], P('mer'), may hold values from 0 to 15, as said below
- ice_mask: int32 [16], P('mer'), may hold values from 0 to 1
Outputs:
- final_state: float32 [2, 2, 64, 1536, 512], P('fluid', None, None, 'zon', 'mer')
The draws below stay inside these ranges and needn't reach their ends.
Inputs may be any that keep to these rules, and one draw needn't show every extreme that they name: `column_solve`: entries of the vertical inverses lie within this range; their diagonal is positive. `block_map`: each meridional section of 4 blocks, blocks k * 4 to (k + 1) * 4 - 1, is mapped onto itself by a permutation.
All inputs are finite; a program needn't handle non-finite values.
Results may differ from the reference program's by a relative error of at most 0.0003.
Values may be sent and summed in bfloat16 or wider, within the bound.
A program may use at most 32 MiB of HBM per device.

```python
import math
import jax
import jax.numpy as jnp
from jax import lax

LEV = 64
TRACERS = 2
BLKW = 32
STEPS = 2
NXZ = 1536
NY = 512
BPD = 4
NYB = 16


def draw_block_map(key, part):
    sections = NYB // BPD
    section_keys = jax.random.split(key, sections)
    shuffled = jax.vmap(lambda sub_key: jax.random.permutation(sub_key, BPD))(section_keys).astype(jnp.int32)
    offsets = (jnp.arange(sections, dtype=jnp.int32) * BPD)[:, None]
    return (shuffled + offsets).reshape(NYB).astype(jnp.int32)


def draw_column_solve(key, part):
    diag_key, scatter_key = jax.random.split(key)
    identity = jnp.eye(LEV, dtype=jnp.float32)
    diagonal = jax.random.uniform(diag_key, (2, LEV), jnp.float32, 0.7, 0.95)
    scatter_part = jnp.clip(jax.random.normal(scatter_key, (2, LEV, LEV), jnp.float32), -2.5, 2.5) * (0.35 * LEV ** (-0.5))
    return (scatter_part * (1.0 - identity) + diagonal[:, :, None] * identity).astype(jnp.float32)


def place_ends(drawn, stream_key, smallest, high):
    index_at = [jax.random.randint(jax.random.fold_in(stream_key, axis), (), 0, length) for axis, length in enumerate(drawn.shape)]
    longest = drawn.shape.index(max(drawn.shape))
    next_to = index_at[:longest] + [(index_at[longest] + 1) % drawn.shape[longest]] + index_at[longest + 1:]
    return drawn.at[tuple(index_at)].set(smallest).at[tuple(next_to)].set(high)


def block_scale(rng, dims, pieces, least, high):
    factor_of, own = 1.0, jax.random.fold_in(rng, 6)
    for dim, blocks in pieces:
        draws = jnp.exp(jax.random.uniform(jax.random.fold_in(own, dim), (blocks,), jnp.float32, least / len(pieces), high / len(pieces)))
        factor_of = factor_of * jnp.repeat(draws, dims[dim] // blocks).reshape([-1 if axis == dim else 1 for axis in range(len(dims))])
    return factor_of


def bell_draw(key, dims, scale, bound, cuts=(), kind=jnp.bfloat16):
    level = block_scale(key, dims, cuts, -0.22, 0.18) if cuts else 1.0
    result = jax.random.normal(key, dims, jnp.float32) * scale * level
    return jnp.minimum(jnp.maximum(result, -bound), bound).astype(kind)


def setup_inputs(seed: int = 0) -> dict:
    key_of = jax.random.split(jax.random.key(seed), 8)
    return {
        "state": bell_draw(key_of[0], (2, TRACERS, LEV, NXZ, NY), 1.0, 6.0, ((0, 2), (3, 96), (4, 4)), jnp.float32),
        "flow": jnp.clip(jax.random.uniform(key_of[1], (2, 2, LEV, NXZ, NY), jnp.float32, -0.5, 0.5) * block_scale(key_of[1], (2, 2, LEV, NXZ, NY), ((0, 2), (3, 96), (4, 4)), -0.4, 0.0), -0.5, 0.5).astype(jnp.bfloat16),
        "diffusion": jnp.clip(jnp.exp(math.log(0.2) - 2.3025851 * jax.random.uniform(key_of[2], (2, TRACERS, LEV), jnp.float32) ** block_scale(key_of[2], (2, TRACERS, LEV), ((0, 2),), -0.2, 0.2)), 0.02, 0.2),
        "column_solve": draw_column_solve(jax.random.fold_in(key_of[7], 71), 0),
        "exchange_rate": jnp.clip(jnp.exp(math.log(0.6) - 1.0986123 * jax.random.uniform(key_of[4], (2, TRACERS), jnp.float32) ** block_scale(key_of[4], (2, TRACERS), ((0, 2),), -0.2, 0.2)), 0.2, 0.6),
        "block_map": draw_block_map(jax.random.fold_in(key_of[7], 71), 0),
        "ice_mask": place_ends(jax.random.randint(key_of[6], (NYB,), 0, 2), jax.random.fold_in(key_of[6], 1), 0, 1).astype(jnp.int32),
    }


def reference(state, flow, diffusion, column_solve, exchange_rate, block_map, ice_mask):
    positions = jnp.arange(NYB, dtype=jnp.int32)
    inverse = jnp.sum(positions[:, None] * (block_map[:, None] == positions[None, :]).astype(jnp.int32), axis=0).astype(jnp.int32)
    open_cols = (1 - ice_mask).astype(jnp.float32)
    level_ids = jnp.arange(LEV, dtype=jnp.int32)
    tracer_field = state
    for step_index in range(STEPS):
        atm_rows = tracer_field[0, :, LEV - 1].reshape(TRACERS, NXZ, NYB, BLKW)
        ocean_rows = tracer_field[1, :, 0].reshape(TRACERS, NXZ, NYB, BLKW)
        mapped = jnp.take(atm_rows, block_map, axis=2)
        surface_flux = (mapped - ocean_rows) * open_cols[None, None, :, None]
        returned = jnp.take(surface_flux, inverse, axis=2)
        increment = jnp.stack([-exchange_rate[0][:, None, None, None] * returned,
                               exchange_rate[1][:, None, None, None] * surface_flux]).reshape(2, TRACERS, NXZ, NY)
        current = tracer_field

        def slab(slab_index):
            fluid_id = slab_index // TRACERS
            tracer_id = slab_index % TRACERS
            tracer_slab = current[fluid_id, tracer_id]
            zonal_flow = flow[fluid_id, 0].astype(jnp.float32)
            merid_flow = flow[fluid_id, 1].astype(jnp.float32)
            viscous = diffusion[fluid_id, tracer_id][:, None, None]
            east_cell = jnp.roll(tracer_slab, -1, axis=1)
            west_cell = jnp.roll(tracer_slab, 1, axis=1)
            padded = jnp.pad(tracer_slab, ((0, 0), (0, 0), (1, 1)))
            north_cell = padded[:, :, 2:]
            south_cell = padded[:, :, :-2]
            updated = (tracer_slab - 0.5 * zonal_flow * (east_cell - west_cell)
                       - 0.5 * merid_flow * (north_cell - south_cell)
                       + viscous * (east_cell + west_cell + north_cell + south_cell - 4.0 * tracer_slab))
            surface_level = jnp.where(fluid_id == 0, LEV - 1, 0).astype(jnp.int32)
            level_pick = (level_ids == surface_level).astype(jnp.float32)
            updated = updated + level_pick[:, None, None] * increment[fluid_id, tracer_id][None]
            solved = jnp.dot(column_solve[fluid_id], updated.reshape(LEV, NXZ * NY),
                             precision=lax.Precision.HIGHEST, preferred_element_type=jnp.float32)
            return solved.reshape(LEV, NXZ, NY)

        tracer_field = lax.map(slab, jnp.arange(2 * TRACERS, dtype=jnp.int32)).reshape(2, TRACERS, LEV, NXZ, NY)
    return tracer_field
```

```python
import jax
import jax.numpy as jnp
from jax import lax
from jax.experimental import pallas as pl
from jax.experimental.pallas import tpu as pltpu
from jax.sharding import PartitionSpec as P

MESH = pl.DeviceIdType.MESH
F32 = jnp.float32
BF16 = jnp.bfloat16
EAST, WEST, NORTH, SOUTH, FLUID = range(5)


def split(value):
    high = value.astype(BF16)
    low = (value - high.astype(F32)).astype(BF16)
    return high, low


def stacked(value):
    high, low = split(value)
    return jnp.concatenate([high, high, low, low], axis=0)


def window_kernel(
    state, rows, flow, diffusion, solve, rate, block_map, ice_mask,
    out,
    q0, q1, res, flow_v, flow_n, half_c, half_d, kappa, diff_v, solve_v, lhs, surf_col,
    rate_s, map_s, ice_s,
    own_surf, other_surf, weights, increment,
    halo_e, halo_w, packed, pack_n, pack_s, flow_p, kappa_p, placed,
    load_sem, small_sem, send_sem, recv_sem, out_sem,
):
    fluid = lax.axis_index("fluid")
    zon = lax.axis_index("zon")
    mer = lax.axis_index("mer")
    zons = lax.axis_size("zon")
    mers = lax.axis_size("mer")
    levels, columns = 64, 16
    peers = (
        (fluid, lax.rem(zon + 1, zons), mer),
        (fluid, lax.rem(zon + zons - 1, zons), mer),
        (fluid, zon, lax.rem(mer + 1, mers)),
        (fluid, zon, lax.rem(mer + mers - 1, mers)),
        (1 - fluid, zon, mer),
    )
    barrier = pltpu.get_barrier_semaphore()
    for peer in peers:
        pl.semaphore_signal(barrier, inc=1, device_id=peer, device_id_type=MESH)

    surface = (levels - 1) * (1 - fluid)
    is_atm = fluid == 0

    smalls = [
        pltpu.make_async_copy(block_map, map_s, small_sem.at[0]),
        pltpu.make_async_copy(ice_mask, ice_s, small_sem.at[1]),
        pltpu.make_async_copy(rate, rate_s, small_sem.at[2]),
        pltpu.make_async_copy(solve, solve_v, small_sem.at[3]),
        pltpu.make_async_copy(diffusion, diff_v, small_sem.at[4]),
        pltpu.make_async_copy(state.at[:, surface], own_surf.at[0], small_sem.at[5]),
    ]
    flow_load = pltpu.make_async_copy(flow, flow_v, load_sem.at[columns])
    flow_load.start()
    loads = []
    for x in range(columns):
        load = pltpu.make_async_copy(rows.at[:, :, x, 0, :], q0.at[x + 1], load_sem.at[x])
        load.start()
        loads.append(load)
    for copy in smalls:
        copy.start()

    pl.semaphore_wait(barrier, 5)

    def send(step, way, source, target):
        slot = step * 5 + way
        copy = pltpu.make_async_remote_copy(
            src_ref=source,
            dst_ref=target,
            send_sem=send_sem.at[slot],
            recv_sem=recv_sem.at[slot],
            device_id=peers[way],
            device_id_type=MESH,
        )
        copy.start()
        return copy

    sends = [{}, {}]
    sends[0][EAST] = send(0, EAST, rows.at[:, :, columns - 1, 0, :], halo_w.at[0])
    sends[0][WEST] = send(0, WEST, rows.at[:, :, 0, 0, :], halo_e.at[0])
    sends[0][FLUID] = send(0, FLUID, state.at[:, surface], other_surf.at[0])

    lane = lax.broadcasted_iota(jnp.int32, (levels, 128), 1)
    lane32 = lax.broadcasted_iota(jnp.int32, (32, 128), 1)
    zero_block = jnp.zeros((2, levels, 128), F32)
    for field in (q0, q1):
        field[0] = zero_block
        field[columns + 1] = zero_block
    for load in loads:
        load.wait()

    def packed_lanes(block, j, total):
        for half in range(2):
            start = 64 * half + 2 * j
            part = block[32 * half : 32 * half + 32]
            total = jnp.where((lane32 >> 1) == (start >> 1), pltpu.roll(part, (start + 1) % 128, 1), total)
        return total

    def pack(field, offset):
        total = jnp.zeros((32, 128), F32)
        for x in range(columns):
            for t in range(2):
                total = packed_lanes(field[x + offset, t], 2 * x + t, total)
        return total

    packed[0] = pack(q0, 1)
    sends[0][NORTH] = send(0, NORTH, packed.at[0], pack_s.at[0])
    sends[0][SOUTH] = send(0, SOUTH, packed.at[0], pack_n.at[0])

    for copy in smalls:
        copy.wait()
    eye = lax.broadcasted_iota(jnp.int32, (levels, levels), 0) == lax.broadcasted_iota(jnp.int32, (levels, levels), 1)
    for t in range(2):
        line = jnp.broadcast_to(diff_v[t : t + 1, :], (levels, levels))
        kappa[t] = jnp.broadcast_to(jnp.sum(jnp.where(eye, line, 0.0), axis=1, keepdims=True), (levels, 128))
    matrix = solve_v[...]
    twice = jnp.concatenate([matrix, matrix], axis=1)
    high = twice.astype(BF16).astype(F32)
    pair = jnp.where(lane < levels, high, twice - high)
    lhs[...] = jnp.concatenate([pair, pair], axis=1).astype(BF16)
    at_surface = lax.broadcasted_iota(jnp.int32, (levels, levels), 1) == surface
    surf_col[...] = jnp.broadcast_to(
        jnp.sum(jnp.where(at_surface, matrix, 0.0), axis=1, keepdims=True), (levels, 128)
    )
    block_of = lax.broadcasted_iota(jnp.int32, (8, 128), 1) // 32
    for k in range(4):
        line = jnp.zeros((8, 128), F32)
        for o in range(4):
            b = (o + k) % 4
            base = 4 * mer
            ocean_hit = jnp.where(map_s[o] - base == b, 1 - ice_s[o], 0)
            atm_hit = jnp.where(map_s[b] - base == o, 1 - ice_s[b], 0)
            hit = jnp.where(is_atm, atm_hit, ocean_hit).astype(F32)
            line = jnp.where(block_of == o, hit, line)
        weights[k] = line

    flow_load.wait()
    for part, half in ((0, half_c), (1, half_d)):
        flow_n[part] = flow_v[part].astype(F32).reshape(levels * columns, 128) * 0.5
        for x in range(columns):
            half[x] = flow_n[part, pl.ds(x, levels, stride=columns), :]
    total = jnp.zeros((32, 128), F32)
    for x in range(columns):
        block = half_d[x]
        for t in range(2):
            total = packed_lanes(block, 2 * x + t, total)
    flow_p[...] = total
    quarter = (lane32 >> 1) & 1
    kappa_p[...] = jnp.where(
        quarter == 0,
        jnp.where(lane32 < 64, kappa[0, 0:32], kappa[0, 32:64]),
        jnp.where(lane32 < 64, kappa[1, 0:32], kappa[1, 32:64]),
    )

    def solve_of(value):
        return jnp.dot(lhs[...], stacked(value), preferred_element_type=F32)

    def interior(field, target, offset):
        def body(x, carry):
            parts = []
            c = half_c[x]
            d = half_d[x]
            for t in range(2):
                k = kappa[t]
                q = field[x + 1, t]
                north = jnp.where(lane == 127, 0.0, pltpu.roll(q, 127, 1))
                south = jnp.where(lane == 0, 0.0, pltpu.roll(q, 1, 1))
                parts.append(
                    (1.0 - 4.0 * k) * q
                    + (k - c) * field[x + 2, t]
                    + (k + c) * field[x, t]
                    + (k - d) * north
                    + (k + d) * south
                )
            solved = solve_of(jnp.concatenate(parts, axis=1))
            target[x + offset, 0] = solved[:, :128]
            target[x + offset, 1] = solved[:, 128:]
            return carry

        lax.fori_loop(0, columns, body, 0, unroll=2)

    def corrections(step, target, offset, first, each):
        sends[step][EAST].wait_recv()
        sends[step][WEST].wait_recv()
        ends = []
        for t in range(2):
            ends.append((kappa[t] + half_c[0]) * halo_w[step, t])
        for t in range(2):
            ends.append((kappa[t] - half_c[columns - 1]) * halo_e[step, t])
        solved_ends = solve_of(jnp.concatenate(ends, axis=1))
        sends[step][FLUID].wait_recv()
        openness = weights[0] + weights[1] + weights[2] + weights[3]
        openness = jnp.concatenate([openness, openness], axis=0)
        for t in range(2):
            other = other_surf[step, t]
            flux = -openness * own_surf[step, t]
            for k in range(4):
                rolled = other if k == 0 else pltpu.roll(other, 128 - 32 * k, 1)
                flux = flux + jnp.concatenate([weights[k], weights[k]], axis=0) * rolled
            increment[step, t] = flux * rate_s[0, t]
        sends[step][NORTH].wait_recv()
        sends[step][SOUTH].wait_recv()
        has_north = jnp.where(mer == mers - 1, 0.0, 1.0)
        has_south = jnp.where(mer == 0, 0.0, 1.0)
        even = (lane32 & 1) == 0
        near = jnp.where(
            even,
            pltpu.roll(pack_n[step], 127, 1) * has_north,
            pltpu.roll(pack_s[step], 1, 1) * has_south,
        )
        terms = (kappa_p[...] + jnp.where(even, -flow_p[...], flow_p[...])) * near
        sides = solve_of(jnp.concatenate([terms, pltpu.roll(terms, 64, 1)], axis=0))
        edge = (lane == 0) | (lane == 127)
        column = surf_col[...]

        def correct(x, extra):
            for t in range(2):
                j = 2 * x + t
                value = target[x + offset, t] + column * increment[step, t, x : x + 1, :]
                value = value + jnp.where(edge, pltpu.roll(sides, (127 - 2 * j) % 128, 1), 0.0)
                if extra is not None:
                    value = value + extra[t]
                target[x + offset, t] = value
            each(x)

        correct(0, (solved_ends[:, 0:128], solved_ends[:, 128:256]))
        correct(columns - 1, (solved_ends[:, 256:384], solved_ends[:, 384:512]))
        first()
        for x in range(1, columns - 1):
            correct(x, None)

    interior(q0, q1, 1)

    def send_ends():
        sends[1][EAST] = send(1, EAST, q1.at[columns], halo_w.at[1])
        sends[1][WEST] = send(1, WEST, q1.at[1], halo_e.at[1])

    def keep_surface(x):
        for t in range(2):
            own_surf[1, t, x : x + 1, :] = q1[x + 1, t, pl.ds(surface, 1), :]

    corrections(0, q1, 1, send_ends, keep_surface)
    sends[1][FLUID] = send(1, FLUID, own_surf.at[1], other_surf.at[1])
    packed[1] = pack(q1, 1)
    sends[1][NORTH] = send(1, NORTH, packed.at[1], pack_s.at[1])
    sends[1][SOUTH] = send(1, SOUTH, packed.at[1], pack_n.at[1])

    interior(q1, res, 0)
    stores = []

    def store(x):
        copy = pltpu.make_async_copy(res.at[x], out.at[:, :, x, 0, :], out_sem.at[x])
        copy.start()
        stores.append(copy)

    corrections(1, res, 0, lambda: None, store)
    for copy in stores:
        copy.wait()
    for step in range(2):
        for way in range(5):
            sends[step][way].wait_send()


def on_device(state, flow, diffusion, column_solve, exchange_rate, block_map, ice_mask):
    _, tracers, levels, columns, merid = state.shape
    local = state.reshape(tracers, levels, columns, merid)
    rows = state.reshape(tracers, levels, columns, 1, merid)
    vmem = pltpu.VMEM
    dma = pltpu.SemaphoreType.DMA
    hbm = pl.BlockSpec(memory_space=pltpu.MemorySpace.HBM)
    result = pl.pallas_call(
        window_kernel,
        out_shape=jax.ShapeDtypeStruct((tracers, levels, columns, 1, merid), F32),
        in_specs=[hbm] * 8,
        out_specs=hbm,
        scratch_shapes=[
            vmem((columns + 2, tracers, levels, merid), F32),
            vmem((columns + 2, tracers, levels, merid), F32),
            vmem((columns, tracers, levels, merid), F32),
            vmem((2, levels, columns, merid), BF16),
            vmem((2, levels * columns, merid), F32),
            vmem((columns, levels, merid), F32),
            vmem((columns, levels, merid), F32),
            vmem((tracers, levels, merid), F32),
            vmem((tracers, levels), F32),
            vmem((levels, levels), F32),
            vmem((levels, 4 * levels), BF16),
            vmem((levels, merid), F32),
            pltpu.SMEM((1, tracers), F32),
            pltpu.SMEM((4,), jnp.int32),
            pltpu.SMEM((4,), jnp.int32),
            vmem((2, tracers, columns, merid), F32),
            vmem((2, tracers, columns, merid), F32),
            vmem((4, 8, merid), F32),
            vmem((2, tracers, columns, merid), F32),
            vmem((2, tracers, levels, merid), F32),
            vmem((2, tracers, levels, merid), F32),
            vmem((2, 32, merid), F32),
            vmem((2, 32, merid), F32),
            vmem((2, 32, merid), F32),
            vmem((32, merid), F32),
            vmem((32, merid), F32),
            vmem((32, merid), F32),
            dma((columns + 1,)),
            dma((6,)),
            dma((10,)),
            dma((10,)),
            dma((columns,)),
        ],
        compiler_params=pltpu.CompilerParams(
            collective_id=0, has_side_effects=True, vmem_limit_bytes=60 * 2**20
        ),
    )(
        local,
        rows,
        flow.reshape(2, levels, columns, merid),
        diffusion.reshape(tracers, levels),
        column_solve.reshape(levels, levels),
        exchange_rate,
        block_map,
        ice_mask,
    )
    return result.reshape(1, tracers, levels, columns, merid)


def solution(mesh):
    return jax.shard_map(
        on_device,
        mesh=mesh,
        in_specs=(
            P("fluid", None, None, "zon", "mer"),
            P("fluid", None, None, "zon", "mer"),
            P("fluid", None, None),
            P("fluid", None, None),
            P("fluid", None),
            P("mer"),
            P("mer"),
        ),
        out_specs=P("fluid", None, None, "zon", "mer"),
        check_vma=False,
    )
```

```python
import jax
import jax.numpy as jnp
from jax import lax
from jax.experimental import pallas as pl
from jax.experimental.pallas import tpu as pltpu
from jax.sharding import PartitionSpec as P

MESH = pl.DeviceIdType.MESH
F32 = jnp.float32
BF16 = jnp.bfloat16


def split(value):
    high = value.astype(BF16)
    low = (value - high.astype(F32)).astype(BF16)
    return high, low


def stacked(value):
    high, low = split(value)
    return jnp.concatenate([high, high, low, low], axis=0)


def window_kernel(
    state, rows, flow, diffusion, solve, rate, block_map, ice_mask,
    res,
    q0, q1, flow_v, flow_n, half_c, half_d, kappa, diff_v, solve_v, lhs, surf_col,
    rate_s, map_s, ice_s,
    own_surf, other_surf, own_late, other_late, west_surf, weights, increment,
    halo_e, west_out, west_in, west_row, ring_out, ring_in,
    mini_out, mini_in, corner_out, corner_n, corner_s,
    pack_out, pack_n, pack_s, pack2_out, pack2_n, pack2_s, flow_p, kappa_p,
    load_sem, small_sem, send_sem, recv_sem,
):
    fluid = lax.axis_index("fluid")
    zon = lax.axis_index("zon")
    mer = lax.axis_index("mer")
    zons = lax.axis_size("zon")
    mers = lax.axis_size("mer")
    levels, columns = 64, 16
    last = columns - 1
    east, west = lax.rem(zon + 1, zons), lax.rem(zon + zons - 1, zons)
    north, south = lax.rem(mer + 1, mers), lax.rem(mer + mers - 1, mers)
    across = 1 - fluid
    barrier = pltpu.get_barrier_semaphore()
    for peer in (
        (fluid, west, mer),
        (fluid, west, north),
        (fluid, west, south),
        (across, west, mer),
        (fluid, zon, north),
        (fluid, zon, south),
        (across, zon, mer),
    ):
        pl.semaphore_signal(barrier, inc=1, device_id=peer, device_id_type=MESH)

    surface = (levels - 1) * (1 - fluid)
    is_atm = fluid == 0

    flow_load = pltpu.make_async_copy(flow, flow_v, load_sem.at[columns])
    flow_load.start()
    loads = []
    for x in range(columns):
        load = pltpu.make_async_copy(rows.at[:, :, x, 0, :], q0.at[x + 1], load_sem.at[x])
        load.start()
        loads.append(load)
    smalls = [
        pltpu.make_async_copy(block_map, map_s, small_sem.at[0]),
        pltpu.make_async_copy(ice_mask, ice_s, small_sem.at[1]),
        pltpu.make_async_copy(rate, rate_s, small_sem.at[2]),
        pltpu.make_async_copy(solve, solve_v, small_sem.at[3]),
        pltpu.make_async_copy(diffusion, diff_v, small_sem.at[4]),
        pltpu.make_async_copy(state.at[:, surface], own_surf.at[0], small_sem.at[5]),
    ]
    for copy in smalls:
        copy.start()

    sent = []

    def copy_to(slot, peer, source, target):
        return pltpu.make_async_remote_copy(
            src_ref=source,
            dst_ref=target,
            send_sem=send_sem.at[slot],
            recv_sem=recv_sem.at[slot],
            device_id=peer,
            device_id_type=MESH,
        )

    row_w = copy_to(0, (fluid, east, mer), west_out, west_in)
    surf_w = copy_to(1, (across, east, mer), rows.at[:, surface, last, 0, :], west_surf)
    surf_0 = copy_to(2, (across, zon, mer), state.at[:, surface], other_surf.at[0])
    corner_to_n = copy_to(3, (fluid, east, north), corner_out, corner_s)
    corner_to_s = copy_to(4, (fluid, east, south), corner_out, corner_n)
    ring = copy_to(5, (fluid, east, mer), ring_out, ring_in)
    mini_w = copy_to(6, (fluid, east, mer), mini_out, mini_in)
    pack_to_n = copy_to(7, (fluid, zon, north), pack_out, pack_s)
    pack_to_s = copy_to(8, (fluid, zon, south), pack_out, pack_n)
    row_e = copy_to(9, (fluid, west, mer), rows.at[:, :, 0, 0, :], halo_e.at[0])
    surf_1 = copy_to(10, (across, zon, mer), own_surf.at[1], other_surf.at[1])
    pack2_to_n = copy_to(11, (fluid, zon, north), pack2_out, pack2_s)
    pack2_to_s = copy_to(12, (fluid, zon, south), pack2_out, pack2_n)
    surf_late = copy_to(13, (across, zon, mer), own_late, other_late)
    row2_e = copy_to(14, (fluid, west, mer), q1.at[1], halo_e.at[1])

    def send(*copies):
        for copy in copies:
            copy.start()
            sent.append(copy)

    lane = lax.broadcasted_iota(jnp.int32, (levels, 128), 1)
    lane32 = lax.broadcasted_iota(jnp.int32, (32, 128), 1)
    even = (lane32 & 1) == 0
    edge = (lane == 0) | (lane == 127)

    def packed_lanes(block, j, total):
        for half in range(2):
            start = 64 * half + 2 * j
            piece = block[32 * half : 32 * half + 32]
            total = jnp.where((lane32 >> 1) == (start >> 1), pltpu.roll(piece, (start + 1) % 128, 1), total)
        return total

    def pack(field):
        total = jnp.zeros((32, 128), F32)
        for x in range(columns):
            for t in range(2):
                total = packed_lanes(field[x + 1, t], 2 * x + t, total)
        return total

    lane8 = lax.broadcasted_iota(jnp.int32, (8, 128), 1)

    def mini(total):
        small = jnp.zeros((8, 128), F32)
        for i in range(4):
            piece = total[8 * i : 8 * i + 8]
            small = jnp.where(((lane8 >> 2) & 15) == 15 - i, pltpu.roll(piece, (128 - 4 * i) % 128, 1), small)
        return small

    def from_mini(small):
        return jnp.concatenate([small] + [pltpu.roll(small, 4 * i, 1) for i in range(1, 4)], axis=0)

    def unpacked(terms):
        return jnp.concatenate([terms, pltpu.roll(terms, 64, 1)], axis=0)

    def at_edges(sides, j):
        return pltpu.roll(sides, (127 - 2 * j) % 128, 1)

    for copy in smalls:
        copy.wait()
    eye = lax.broadcasted_iota(jnp.int32, (levels, levels), 0) == lax.broadcasted_iota(jnp.int32, (levels, levels), 1)
    for t in range(2):
        line = jnp.broadcast_to(diff_v[t : t + 1, :], (levels, levels))
        kappa[t] = jnp.broadcast_to(jnp.sum(jnp.where(eye, line, 0.0), axis=1, keepdims=True), (levels, 128))
    matrix = solve_v[...]
    twice = jnp.concatenate([matrix, matrix], axis=1)
    high = twice.astype(BF16).astype(F32)
    pair = jnp.where(lane < levels, high, twice - high)
    lhs[...] = jnp.concatenate([pair, pair], axis=1).astype(BF16)
    at_surface = lax.broadcasted_iota(jnp.int32, (levels, levels), 1) == surface
    surf_col[...] = jnp.broadcast_to(
        jnp.sum(jnp.where(at_surface, matrix, 0.0), axis=1, keepdims=True), (levels, 128)
    )
    quarter = (lane32 >> 1) & 1
    kappa_p[...] = jnp.where(
        quarter == 0,
        jnp.where(lane32 < 64, kappa[0, 0:32], kappa[0, 32:64]),
        jnp.where(lane32 < 64, kappa[1, 0:32], kappa[1, 32:64]),
    )
    zero_block = jnp.zeros((2, levels, 128), F32)
    for field in (q0, q1):
        field[0] = zero_block
        field[columns + 1] = zero_block

    flow_load.wait()
    for piece, half in ((0, half_c), (1, half_d)):
        flow_n[piece] = flow_v[piece].astype(F32).reshape(levels * columns, 128) * 0.5
        for x in range(columns):
            half[x] = flow_n[piece, pl.ds(x, levels, stride=columns), :]
    total = jnp.zeros((32, 128), F32)
    for x in range(columns):
        block = half_d[x]
        for t in range(2):
            total = packed_lanes(block, 2 * x + t, total)
    flow_p[...] = total
    mini_out[...] = mini(total)
    ring_out[0] = half_c[last].astype(BF16)
    for load in loads:
        load.wait()

    def solve_of(value):
        return jnp.dot(lhs[...], stacked(value), preferred_element_type=F32)

    def interior(field, target, offset, x):
        c = half_c[x]
        d = half_d[x]
        parts = []
        for t in range(2):
            k = kappa[t]
            q = field[x + 1, t]
            parts.append(
                (1.0 - 4.0 * k) * q
                + (k - c) * field[x + 2, t]
                + (k + c) * field[x, t]
                + (k - d) * jnp.where(lane == 127, 0.0, pltpu.roll(q, 127, 1))
                + (k + d) * jnp.where(lane == 0, 0.0, pltpu.roll(q, 1, 1))
            )
        solved = solve_of(jnp.concatenate(parts, axis=1))
        target[x + offset, 0] = solved[:, :128]
        target[x + offset, 1] = solved[:, 128:]

    interior(q0, q1, 1, last)
    ring_out[1:3] = q1[columns].astype(BF16)
    west_out[...] = q0[columns].astype(BF16)
    total = pack(q0)
    pack_out[0:32] = total
    corner_out[...] = mini(total)
    ends = jnp.zeros((32, 128), F32)
    for t in range(2):
        ends = packed_lanes(half_c[0], 2 * last + t, ends)
    pack_out[32:40] = mini(ends)

    pl.semaphore_wait(barrier, 7)
    send(row_w, ring, mini_w, corner_to_n, corner_to_s, surf_w, surf_0, pack_to_n, pack_to_s)

    block_of = lax.broadcasted_iota(jnp.int32, (8, 128), 1) // 32
    base = 4 * mer
    for k in range(4):
        line = jnp.zeros((8, 128), F32)
        for o in range(4):
            b = (o + k) % 4
            ocean_hit = jnp.where(map_s[o] - base == b, 1 - ice_s[o], 0)
            atm_hit = jnp.where(map_s[b] - base == o, 1 - ice_s[b], 0)
            hit = jnp.where(is_atm, atm_hit, ocean_hit).astype(F32)
            line = jnp.where(block_of == o, hit, line)
        weights[k] = line

    def first_body(x, carry):
        interior(q0, q1, 1, x)
        return carry

    lax.fori_loop(0, last, first_body, 0, unroll=3)

    def exchange(own, other, repeat):
        shares = [jnp.concatenate([weights[k]] * repeat, axis=0) if repeat else weights[k][0:2] for k in range(4)]
        flux = -(shares[0] + shares[1] + shares[2] + shares[3]) * own
        for k in range(4):
            flux = flux + shares[k] * (other if k == 0 else pltpu.roll(other, 128 - 32 * k, 1))
        return flux

    def increments(step):
        for t in range(2):
            increment[step, t] = exchange(own_surf[step, t], other_surf[step, t], 2) * rate_s[0, t]

    has_north = jnp.where(mer == mers - 1, 0.0, 1.0)
    has_south = jnp.where(mer == 0, 0.0, 1.0)

    def near(from_n, from_s):
        return jnp.where(even, pltpu.roll(from_n, 127, 1) * has_north, pltpu.roll(from_s, 1, 1) * has_south)

    def side_terms(beyond, half):
        return (kappa_p[...] + jnp.where(even, -half, half)) * beyond

    def greet_west():
        row_w.wait_recv()
        row_e.start()

    sent.append(row_e)
    seam = lax.rem(zon, 24) == 0
    pl.when(jnp.logical_not(seam))(greet_west)

    surf_0.wait_recv()
    increments(0)
    pack_to_n.wait_recv()
    pack_to_s.wait_recv()
    sides = solve_of(unpacked(side_terms(near(pack_n[0:32], pack_s[0:32]), flow_p[...])))
    column = surf_col[...]

    def corrected(step, target, offset, x):
        return [
            target[x + offset, t]
            + column * increment[step, t, x : x + 1, :]
            + jnp.where(edge, at_edges(sides, 2 * x + t), 0.0)
            for t in range(2)
        ]

    def keep(x, values):
        for t in range(2):
            q1[x + 1, t] = values[t]
            own_surf[1, t, x : x + 1, :] = q1[x + 1, t, pl.ds(surface, 1), :]

    for x in range(last):
        keep(x, corrected(0, q1, 1, x))
    row_e.wait_recv()
    k_c = [kappa[t] - half_c[last] for t in range(2)]
    solved = solve_of(jnp.concatenate([k_c[t] * halo_e[0, t] for t in range(2)], axis=1))
    values = corrected(0, q1, 1, last)
    keep(last, [values[0] + solved[:, :128], values[1] + solved[:, 128:]])
    send(surf_1)
    pack2_out[...] = pack(q1)
    send(pack2_to_n, pack2_to_s)

    def second_body(x, carry):
        interior(q1, res, 0, x)
        return carry

    lax.fori_loop(2, columns, second_body, 0, unroll=2)
    surf_1.wait_recv()
    increments(1)
    pack2_to_n.wait_recv()
    pack2_to_s.wait_recv()
    beyond = near(pack2_n[...], pack2_s[...])
    sides = solve_of(unpacked(side_terms(beyond, flow_p[...])))
    for x in range(2, columns):
        values = corrected(1, res, 0, x)
        for t in range(2):
            res[x, t] = values[t]
    beyond = unpacked(beyond)

    pl.when(seam)(greet_west)
    ring.wait_recv()
    mini_w.wait_recv()
    corner_to_n.wait_recv()
    corner_to_s.wait_recv()
    west_row[...] = west_in[...].astype(F32)
    k_c = [kappa[t] + half_c[0] for t in range(2)]
    k_w = [kappa[t] - ring_in[0].astype(F32) for t in range(2)]
    from_n = from_mini(corner_n[...])
    from_s = from_mini(corner_s[...])
    corners = side_terms(near(from_n, from_s), from_mini(mini_in[...]))
    mixed = jnp.where(
        even,
        (kappa_p[...] + from_mini(pack_s[32:40])) * from_s * has_south,
        (kappa_p[...] + from_mini(pack_n[32:40])) * from_n * has_north,
    )
    solved = solve_of(
        jnp.concatenate(
            [k_c[t] * west_row[t] for t in range(2)]
            + [k_w[t] * q0[1, t] for t in range(2)]
            + [unpacked(corners), unpacked(mixed)],
            axis=1,
        )
    )
    pieces = [solved[:, 128 * i : 128 * i + 128] for i in range(6)]
    firsts = [q1[1, t] + pieces[t] for t in range(2)]
    for t in range(2):
        q1[1, t] = firsts[t]
        own_late[t : t + 1, :] = q1[1, t, pl.ds(surface, 1), :]
    send(surf_late, row2_e)
    shift = jnp.where((lane & 1) == 0, pltpu.roll(pieces[5], 67, 1), pltpu.roll(pieces[5], 69, 1))
    beyond_first = beyond + shift
    tracer = lax.broadcasted_iota(jnp.int32, (2, 128), 0)
    rates = jnp.where(tracer == 0, rate_s[0, 0], rate_s[0, 1])
    surf_w.wait_recv()
    west_own = jnp.concatenate([west_row[t, pl.ds(surface, 1), :] for t in range(2)], axis=0)
    west_flux = exchange(west_own, west_surf[...], 0) * rates
    wests = [
        ring_in[1 + t].astype(F32)
        + pieces[2 + t]
        + column * west_flux[t : t + 1]
        + jnp.where(edge, at_edges(pieces[4], 2 * last + t), 0.0)
        for t in range(2)
    ]

    def full(k, c, d, q, to_east, to_west, around):
        return (
            (1.0 - 4.0 * k) * q
            + (k - c) * to_east
            + (k + c) * to_west
            + (k - d) * jnp.where(lane == 127, around, pltpu.roll(q, 127, 1))
            + (k + d) * jnp.where(lane == 0, around, pltpu.roll(q, 1, 1))
        )

    updates = [
        full(kappa[t], half_c[0], half_d[0], firsts[t], q1[2, t], wests[t], at_edges(beyond_first, t)) for t in range(2)
    ] + [
        full(kappa[t], half_c[1], half_d[1], q1[2, t], q1[3, t], firsts[t], at_edges(beyond, 2 + t)) for t in range(2)
    ]
    solved = solve_of(jnp.concatenate(updates, axis=1))
    for t in range(2):
        res[1, t] = solved[:, 256 + 128 * t : 384 + 128 * t] + column * increment[1, t, 1:2, :]
    surf_late.wait_recv()
    late_flux = exchange(own_late[...], other_late[...], 0) * rates
    for t in range(2):
        res[0, t] = solved[:, 128 * t : 128 * t + 128] + column * late_flux[t : t + 1]

    row2_e.wait_recv()
    solved = solve_of(
        jnp.concatenate([(kappa[t] - half_c[last]) * halo_e[1, t] for t in range(2)], axis=1)
    )
    for t in range(2):
        res[last, t] = res[last, t] + solved[:, 128 * t : 128 * t + 128]
    for copy in sent:
        copy.wait_send()


def finish_kernel(source, out, sem):
    copies = [pltpu.make_async_copy(source.at[x], out.at[:, :, x, 0, :], sem.at[x]) for x in range(16)]
    for copy in copies:
        copy.start()
    for copy in copies:
        copy.wait()


def on_device(state, flow, diffusion, column_solve, exchange_rate, block_map, ice_mask):
    _, tracers, levels, columns, merid = state.shape
    local = state.reshape(tracers, levels, columns, merid)
    rows = state.reshape(tracers, levels, columns, 1, merid)
    vmem = pltpu.VMEM
    dma = pltpu.SemaphoreType.DMA
    hbm = pl.BlockSpec(memory_space=pltpu.MemorySpace.HBM)
    result = pl.pallas_call(
        window_kernel,
        out_shape=jax.ShapeDtypeStruct((columns, tracers, levels, merid), F32),
        in_specs=[hbm] * 8,
        out_specs=pl.BlockSpec(memory_space=pltpu.VMEM),
        scratch_shapes=[
            vmem((columns + 2, tracers, levels, merid), F32),
            vmem((columns + 2, tracers, levels, merid), F32),
            vmem((2, levels, columns, merid), BF16),
            vmem((2, levels * columns, merid), F32),
            vmem((columns, levels, merid), F32),
            vmem((columns, levels, merid), F32),
            vmem((tracers, levels, merid), F32),
            vmem((tracers, levels), F32),
            vmem((levels, levels), F32),
            vmem((levels, 4 * levels), BF16),
            vmem((levels, merid), F32),
            pltpu.SMEM((1, tracers), F32),
            pltpu.SMEM((4,), jnp.int32),
            pltpu.SMEM((4,), jnp.int32),
            vmem((2, tracers, columns, merid), F32),
            vmem((2, tracers, columns, merid), F32),
            vmem((tracers, merid), F32),
            vmem((tracers, merid), F32),
            vmem((tracers, merid), F32),
            vmem((4, 8, merid), F32),
            vmem((2, tracers, columns, merid), F32),
            vmem((2, tracers, levels, merid), F32),
            vmem((tracers, levels, merid), BF16),
            vmem((tracers, levels, merid), BF16),
            vmem((tracers, levels, merid), F32),
            vmem((tracers + 1, levels, merid), BF16),
            vmem((tracers + 1, levels, merid), BF16),
        ]
        + [vmem((8, merid), F32)] * 5
        + [vmem((40, merid), F32)] * 3
        + [vmem((32, merid), F32)] * 5
        + [
            dma((columns + 1,)),
            dma((6,)),
            dma((15,)),
            dma((15,)),
        ],
        compiler_params=pltpu.CompilerParams(
            collective_id=0, has_side_effects=True, vmem_limit_bytes=48 * 2**20
        ),
    )(
        *(pltpu.with_memory_space_constraint(v, pltpu.MemorySpace.HBM) for v in (
        local,
        rows,
        flow.reshape(2, levels, columns, merid),
        diffusion.reshape(tracers, levels),
        column_solve.reshape(levels, levels),
        exchange_rate,
        block_map,
        ice_mask,
    )))
    result = pl.pallas_call(
        finish_kernel,
        out_shape=jax.ShapeDtypeStruct((tracers, levels, columns, 1, merid), F32),
        in_specs=[pl.BlockSpec(memory_space=pltpu.VMEM)],
        out_specs=hbm,
        scratch_shapes=[dma((16,))],
        compiler_params=pltpu.CompilerParams(vmem_limit_bytes=48 * 2**20),
    )(result)
    return result.reshape(1, tracers, levels, columns, merid)


def solution(mesh):
    return jax.shard_map(
        on_device,
        mesh=mesh,
        in_specs=(
            P("fluid", None, None, "zon", "mer"),
            P("fluid", None, None, "zon", "mer"),
            P("fluid", None, None),
            P("fluid", None, None),
            P("fluid", None),
            P("mer"),
            P("mer"),
        ),
        out_specs=P("fluid", None, None, "zon", "mer"),
        check_vma=False,
    )
```

```python
import jax
import jax.numpy as jnp
from jax import lax
from jax.experimental import pallas as pl
from jax.experimental.pallas import tpu as pltpu
from jax.sharding import PartitionSpec as P

MESH = pl.DeviceIdType.MESH
F32 = jnp.float32
BF16 = jnp.bfloat16


def split(value):
    high = value.astype(BF16)
    low = (value - high.astype(F32)).astype(BF16)
    return high, low


def stacked(value):
    high, low = split(value)
    return jnp.concatenate([high, high, low, low], axis=0)


def window_kernel(
    state, rows, flow, diffusion, solve, rate, block_map, ice_mask,
    res,
    q0, q1, flow_v, flow_n, half_c, half_d, kappa, diff_v, solve_v, lhs, surf_col,
    rate_s, map_s, ice_s,
    own_surf, other_surf, own_late, other_late, west_surf, weights, increment,
    halo_e, west_out, west_in, west_row, ring_out, ring_in, wests, corner_shift,
    mini_out, mini_in, corner_out, corner_n, corner_s,
    pack_out, pack_n, pack_s, pack2_out, pack2_n, pack2_s, flow_p, kappa_p,
    load_sem, small_sem, send_sem, recv_sem, token,
):
    fluid = lax.axis_index("fluid")
    zon = lax.axis_index("zon")
    mer = lax.axis_index("mer")
    zons = lax.axis_size("zon")
    mers = lax.axis_size("mer")
    levels, columns = 64, 16
    last = columns - 1
    east, west = lax.rem(zon + 1, zons), lax.rem(zon + zons - 1, zons)
    north, south = lax.rem(mer + 1, mers), lax.rem(mer + mers - 1, mers)
    across = 1 - fluid
    barrier = pltpu.get_barrier_semaphore()

    def greet(peers):
        for peer in peers:
            pl.semaphore_signal(barrier, inc=1, device_id=peer, device_id_type=MESH)

    before_seam = lax.rem(zon, 24) == 23
    after_seam = lax.rem(zon, 24) == 0
    greet(((fluid, west, mer), (fluid, west, north), (fluid, west, south), (across, west, mer)))

    @pl.when(jnp.logical_not(before_seam))
    def _():
        greet(((fluid, zon, north), (fluid, zon, south), (across, zon, mer)))

    surface = (levels - 1) * (1 - fluid)
    is_atm = fluid == 0

    loads = [pltpu.make_async_copy(rows.at[:, :, x, 0, :], q0.at[x + 1], load_sem.at[x]) for x in range(columns)]
    loads[last].start()
    flow_load = pltpu.make_async_copy(flow, flow_v, load_sem.at[columns])
    flow_load.start()
    smalls = [
        pltpu.make_async_copy(block_map, map_s, small_sem.at[0]),
        pltpu.make_async_copy(ice_mask, ice_s, small_sem.at[1]),
        pltpu.make_async_copy(rate, rate_s, small_sem.at[2]),
        pltpu.make_async_copy(solve, solve_v, small_sem.at[3]),
        pltpu.make_async_copy(diffusion, diff_v, small_sem.at[4]),
        pltpu.make_async_copy(state.at[:, surface], own_surf.at[0], small_sem.at[5]),
    ]
    for copy in smalls:
        copy.start()
    for x in (last - 1, *range(last - 1)):
        loads[x].start()

    def copy_to(slot, peer, source, target):
        return pltpu.make_async_remote_copy(
            src_ref=source,
            dst_ref=target,
            send_sem=send_sem.at[slot],
            recv_sem=recv_sem.at[slot],
            device_id=peer,
            device_id_type=MESH,
        )

    row_w = copy_to(0, (fluid, east, mer), west_out, west_in)
    surf_w = copy_to(1, (across, east, mer), rows.at[:, surface, last, 0, :], west_surf)
    surf_0 = copy_to(2, (across, zon, mer), state.at[:, surface], other_surf.at[0])
    corner_to_n = copy_to(3, (fluid, east, north), corner_out, corner_s)
    corner_to_s = copy_to(4, (fluid, east, south), corner_out, corner_n)
    ring = copy_to(5, (fluid, east, mer), ring_out, ring_in)
    mini_w = copy_to(6, (fluid, east, mer), mini_out, mini_in)
    pack_to_n = copy_to(7, (fluid, zon, north), pack_out, pack_s)
    pack_to_s = copy_to(8, (fluid, zon, south), pack_out, pack_n)
    row_e = copy_to(9, (fluid, west, mer), rows.at[:, :, 0, 0, :], halo_e.at[0])
    surf_1 = copy_to(10, (across, zon, mer), own_surf.at[1], other_surf.at[1])
    pack2_to_n = copy_to(11, (fluid, zon, north), pack2_out, pack2_s)
    pack2_to_s = copy_to(12, (fluid, zon, south), pack2_out, pack2_n)
    surf_late = copy_to(13, (across, zon, mer), own_late, other_late)
    row2_e = copy_to(14, (fluid, west, mer), q1.at[1], halo_e.at[1])

    def send(*copies):
        for copy in copies:
            copy.start()

    def send_before_seam(*copies):
        pl.when(before_seam)(lambda: send(*copies))

    @pl.when(before_seam)
    def _():
        pl.semaphore_wait(barrier, 4)
        send(surf_w)

    lane = lax.broadcasted_iota(jnp.int32, (levels, 128), 1)
    lane32 = lax.broadcasted_iota(jnp.int32, (32, 128), 1)
    even = (lane32 & 1) == 0
    edge = (lane == 0) | (lane == 127)

    def packed_lanes(block, j, total):
        for half in range(2):
            start = 64 * half + 2 * j
            piece = block[32 * half : 32 * half + 32]
            total = jnp.where((lane32 >> 1) == (start >> 1), pltpu.roll(piece, (start + 1) % 128, 1), total)
        return total

    def pack(field):
        total = jnp.zeros((32, 128), F32)
        for x in range(columns):
            for t in range(2):
                total = packed_lanes(field[x + 1, t], 2 * x + t, total)
        return total

    lane8 = lax.broadcasted_iota(jnp.int32, (8, 128), 1)

    def mini(total):
        small = jnp.zeros((8, 128), F32)
        for i in range(4):
            piece = total[8 * i : 8 * i + 8]
            small = jnp.where(((lane8 >> 2) & 15) == 15 - i, pltpu.roll(piece, (128 - 4 * i) % 128, 1), small)
        return small

    def from_mini(small):
        return jnp.concatenate([small] + [pltpu.roll(small, 4 * i, 1) for i in range(1, 4)], axis=0)

    def unpacked(terms):
        return jnp.concatenate([terms, pltpu.roll(terms, 64, 1)], axis=0)

    def at_edges(sides, j):
        return pltpu.roll(sides, (127 - 2 * j) % 128, 1)

    loads[last].wait()
    west_out[...] = q0[columns].astype(BF16)
    total = jnp.zeros((32, 128), F32)
    for t in range(2):
        total = packed_lanes(q0[columns, t], 2 * last + t, total)
    corner_out[...] = mini(total)
    send_before_seam(corner_to_n, corner_to_s, row_w)

    for copy in smalls:
        copy.wait()
    eye = lax.broadcasted_iota(jnp.int32, (levels, levels), 0) == lax.broadcasted_iota(jnp.int32, (levels, levels), 1)
    for t in range(2):
        line = jnp.broadcast_to(diff_v[t : t + 1, :], (levels, levels))
        kappa[t] = jnp.broadcast_to(jnp.sum(jnp.where(eye, line, 0.0), axis=1, keepdims=True), (levels, 128))
    matrix = solve_v[...]
    twice = jnp.concatenate([matrix, matrix], axis=1)
    high = twice.astype(BF16).astype(F32)
    pair = jnp.where(lane < levels, high, twice - high)
    lhs[...] = jnp.concatenate([pair, pair], axis=1).astype(BF16)
    at_surface = lax.broadcasted_iota(jnp.int32, (levels, levels), 1) == surface
    surf_col[...] = jnp.broadcast_to(
        jnp.sum(jnp.where(at_surface, matrix, 0.0), axis=1, keepdims=True), (levels, 128)
    )
    quarter = (lane32 >> 1) & 1
    kappa_p[...] = jnp.where(
        quarter == 0,
        jnp.where(lane32 < 64, kappa[0, 0:32], kappa[0, 32:64]),
        jnp.where(lane32 < 64, kappa[1, 0:32], kappa[1, 32:64]),
    )
    zero_block = jnp.zeros((2, levels, 128), F32)
    for field in (q0, q1):
        field[0] = zero_block
        field[columns + 1] = zero_block

    def solve_of(value):
        return jnp.dot(lhs[...], stacked(value), preferred_element_type=F32)

    def interior(field, target, offset, x):
        c = half_c[x]
        d = half_d[x]
        parts = []
        for t in range(2):
            k = kappa[t]
            q = field[x + 1, t]
            parts.append(
                (1.0 - 4.0 * k) * q
                + (k - c) * field[x + 2, t]
                + (k + c) * field[x, t]
                + (k - d) * jnp.where(lane == 127, 0.0, pltpu.roll(q, 127, 1))
                + (k + d) * jnp.where(lane == 0, 0.0, pltpu.roll(q, 1, 1))
            )
        solved = solve_of(jnp.concatenate(parts, axis=1))
        target[x + offset, 0] = solved[:, :128]
        target[x + offset, 1] = solved[:, 128:]

    flow_load.wait()
    for piece in range(2):
        flow_n[piece] = flow_v[piece].astype(F32).reshape(levels * columns, 128) * 0.5

    def turn(x):
        half_c[x] = flow_n[0, pl.ds(x, levels, stride=columns), :]
        half_d[x] = flow_n[1, pl.ds(x, levels, stride=columns), :]

    turn(last)
    total = jnp.zeros((32, 128), F32)
    for t in range(2):
        total = packed_lanes(half_d[last], 2 * last + t, total)
    mini_out[...] = mini(total)
    loads[last - 1].wait()
    interior(q0, q1, 1, last)
    ring_out[0] = half_c[last].astype(BF16)
    ring_out[1:3] = q1[columns].astype(BF16)
    send_before_seam(ring, mini_w)

    for x in range(last):
        turn(x)
        for t in range(2):
            total = packed_lanes(half_d[x], 2 * x + t, total)
    flow_p[...] = total
    for x in range(last - 1):
        loads[x].wait()
    pack_out[0:32] = pack(q0)
    ends = jnp.zeros((32, 128), F32)
    for t in range(2):
        ends = packed_lanes(half_c[0], 2 * last + t, ends)
    pack_out[32:40] = mini(ends)

    @pl.when(jnp.logical_not(before_seam))
    def _():
        pl.semaphore_wait(barrier, 7)
        send(corner_to_n, corner_to_s, row_w, ring, mini_w, surf_w, surf_0, pack_to_n, pack_to_s)

    block_of = lax.broadcasted_iota(jnp.int32, (8, 128), 1) // 32
    base = 4 * mer
    for k in range(4):
        line = jnp.zeros((8, 128), F32)
        for o in range(4):
            b = (o + k) % 4
            ocean_hit = jnp.where(map_s[o] - base == b, 1 - ice_s[o], 0)
            atm_hit = jnp.where(map_s[b] - base == o, 1 - ice_s[b], 0)
            hit = jnp.where(is_atm, atm_hit, ocean_hit).astype(F32)
            line = jnp.where(block_of == o, hit, line)
        weights[k] = line

    def first_body(x, carry):
        interior(q0, q1, 1, x)
        return carry

    lax.fori_loop(0, last, first_body, 0, unroll=3)

    def exchange(own, other, repeat):
        shares = [jnp.concatenate([weights[k]] * repeat, axis=0) if repeat else weights[k][0:2] for k in range(4)]
        flux = -(shares[0] + shares[1] + shares[2] + shares[3]) * own
        for k in range(4):
            flux = flux + shares[k] * (other if k == 0 else pltpu.roll(other, 128 - 32 * k, 1))
        return flux

    def increments(step):
        for t in range(2):
            increment[step, t] = exchange(own_surf[step, t], other_surf[step, t], 2) * rate_s[0, t]

    has_north = jnp.where(mer == mers - 1, 0.0, 1.0)
    has_south = jnp.where(mer == 0, 0.0, 1.0)

    def near(from_n, from_s):
        return jnp.where(even, pltpu.roll(from_n, 127, 1) * has_north, pltpu.roll(from_s, 1, 1) * has_south)

    def side_terms(beyond, half):
        return (kappa_p[...] + jnp.where(even, -half, half)) * beyond

    @pl.when(jnp.logical_not(after_seam))
    def _():
        row_w.wait_recv()
        row_e.start()

    @pl.when(before_seam)
    def _():
        row_e.wait_recv()
        pl.semaphore_wait(token, 1)
        send(surf_0, pack_to_n, pack_to_s)

    surf_0.wait_recv()
    increments(0)
    pack_to_n.wait_recv()
    pack_to_s.wait_recv()
    sides = solve_of(unpacked(side_terms(near(pack_n[0:32], pack_s[0:32]), flow_p[...])))
    column = surf_col[...]

    def corrected(step, target, offset, x):
        return [
            target[x + offset, t]
            + column * increment[step, t, x : x + 1, :]
            + jnp.where(edge, at_edges(sides, 2 * x + t), 0.0)
            for t in range(2)
        ]

    def keep(x, values):
        for t in range(2):
            q1[x + 1, t] = values[t]
            own_surf[1, t, x : x + 1, :] = q1[x + 1, t, pl.ds(surface, 1), :]

    for x in range(last):
        keep(x, corrected(0, q1, 1, x))
    pl.when(jnp.logical_not(before_seam))(row_e.wait_recv)
    k_c = [kappa[t] - half_c[last] for t in range(2)]
    solved = solve_of(jnp.concatenate([k_c[t] * halo_e[0, t] for t in range(2)], axis=1))
    values = corrected(0, q1, 1, last)
    keep(last, [values[0] + solved[:, :128], values[1] + solved[:, 128:]])
    send(surf_1)
    pack2_out[...] = pack(q1)
    send(pack2_to_n, pack2_to_s)

    def west_side(late):
        if late:
            row_w.wait_recv()
            corner_to_n.wait_recv()
            surf_w.wait_recv()
            row_e.start()
            pl.semaphore_signal(token, inc=1, device_id=(fluid, west, south), device_id_type=MESH)
        west_row[...] = west_in[...].astype(F32)
        solved = solve_of(jnp.concatenate([(kappa[t] + half_c[0]) * west_row[t] for t in range(2)], axis=1))
        for t in range(2):
            q1[1, t] = q1[1, t] + solved[:, 128 * t : 128 * t + 128]
            own_late[t : t + 1, :] = q1[1, t, pl.ds(surface, 1), :]
        send(surf_late, row2_e)
        ring.wait_recv()
        k_w = [kappa[t] - ring_in[0].astype(F32) for t in range(2)]
        own = solve_of(jnp.concatenate([k_w[t] * q0[1, t] for t in range(2)], axis=1))
        if not late:
            surf_w.wait_recv()
        west_own = jnp.concatenate([west_row[t, pl.ds(surface, 1), :] for t in range(2)], axis=0)
        west_flux = exchange(west_own, west_surf[...], 0) * rates
        for t in range(2):
            wests[t] = (
                ring_in[1 + t].astype(F32) + own[:, 128 * t : 128 * t + 128] + column * west_flux[t : t + 1]
            )

    def west_corners(late):
        mini_w.wait_recv()
        if not late:
            corner_to_n.wait_recv()
        corner_to_s.wait_recv()
        from_n = from_mini(corner_n[...])
        from_s = from_mini(corner_s[...])
        corners = side_terms(near(from_n, from_s), from_mini(mini_in[...]))
        mixed = jnp.where(
            even,
            (kappa_p[...] + from_mini(pack_s[32:40])) * from_s * has_south,
            (kappa_p[...] + from_mini(pack_n[32:40])) * from_n * has_north,
        )
        solved = solve_of(jnp.concatenate([unpacked(corners), unpacked(mixed)], axis=1))
        for t in range(2):
            wests[t] = wests[t] + jnp.where(edge, at_edges(solved[:, 0:128], 2 * last + t), 0.0)
        mixed = solved[:, 128:256]
        corner_shift[...] = jnp.where((lane & 1) == 0, pltpu.roll(mixed, 67, 1), pltpu.roll(mixed, 69, 1))

    tracer = lax.broadcasted_iota(jnp.int32, (2, 128), 0)
    rates = jnp.where(tracer == 0, rate_s[0, 0], rate_s[0, 1])

    @pl.when(jnp.logical_not(after_seam))
    def _():
        west_side(False)
        west_corners(False)

    def second_body(x, carry):
        interior(q1, res, 0, x)
        return carry

    lax.fori_loop(2, columns, second_body, 0, unroll=2)
    pl.when(after_seam)(lambda: west_side(True))
    surf_1.wait_recv()
    increments(1)
    pack2_to_n.wait_recv()
    pack2_to_s.wait_recv()
    beyond = near(pack2_n[...], pack2_s[...])
    sides = solve_of(unpacked(side_terms(beyond, flow_p[...])))
    for x in range(2, columns):
        values = corrected(1, res, 0, x)
        for t in range(2):
            res[x, t] = values[t]
    beyond = unpacked(beyond)

    pl.when(after_seam)(lambda: west_corners(True))
    firsts = [q1[1, t] for t in range(2)]
    beyond_first = beyond + corner_shift[...]

    def full(k, c, d, q, to_east, to_west, around):
        return (
            (1.0 - 4.0 * k) * q
            + (k - c) * to_east
            + (k + c) * to_west
            + (k - d) * jnp.where(lane == 127, around, pltpu.roll(q, 127, 1))
            + (k + d) * jnp.where(lane == 0, around, pltpu.roll(q, 1, 1))
        )

    updates = [
        full(kappa[t], half_c[0], half_d[0], firsts[t], q1[2, t], wests[t], at_edges(beyond_first, t)) for t in range(2)
    ] + [
        full(kappa[t], half_c[1], half_d[1], q1[2, t], q1[3, t], firsts[t], at_edges(beyond, 2 + t)) for t in range(2)
    ]
    solved = solve_of(jnp.concatenate(updates, axis=1))
    for t in range(2):
        res[1, t] = solved[:, 256 + 128 * t : 384 + 128 * t] + column * increment[1, t, 1:2, :]
    surf_late.wait_recv()
    late_flux = exchange(own_late[...], other_late[...], 0) * rates
    for t in range(2):
        res[0, t] = solved[:, 128 * t : 128 * t + 128] + column * late_flux[t : t + 1]

    row2_e.wait_recv()
    solved = solve_of(
        jnp.concatenate([(kappa[t] - half_c[last]) * halo_e[1, t] for t in range(2)], axis=1)
    )
    for t in range(2):
        res[last, t] = res[last, t] + solved[:, 128 * t : 128 * t + 128]
    for copy in (
        row_w, surf_w, surf_0, corner_to_n, corner_to_s, ring, mini_w, pack_to_n,
        pack_to_s, row_e, surf_1, pack2_to_n, pack2_to_s, surf_late, row2_e,
    ):
        copy.wait_send()


def finish_kernel(source, out, sem):
    copies = [pltpu.make_async_copy(source.at[x], out.at[:, :, x, 0, :], sem.at[x]) for x in range(16)]
    for copy in copies:
        copy.start()
    for copy in copies:
        copy.wait()


def on_device(state, flow, diffusion, column_solve, exchange_rate, block_map, ice_mask):
    _, tracers, levels, columns, merid = state.shape
    local = state.reshape(tracers, levels, columns, merid)
    rows = state.reshape(tracers, levels, columns, 1, merid)
    vmem = pltpu.VMEM
    dma = pltpu.SemaphoreType.DMA
    hbm = pl.BlockSpec(memory_space=pltpu.MemorySpace.HBM)
    result = pl.pallas_call(
        window_kernel,
        out_shape=jax.ShapeDtypeStruct((columns, tracers, levels, merid), F32),
        in_specs=[hbm] * 8,
        out_specs=pl.BlockSpec(memory_space=pltpu.VMEM),
        scratch_shapes=[
            vmem((columns + 2, tracers, levels, merid), F32),
            vmem((columns + 2, tracers, levels, merid), F32),
            vmem((2, levels, columns, merid), BF16),
            vmem((2, levels * columns, merid), F32),
            vmem((columns, levels, merid), F32),
            vmem((columns, levels, merid), F32),
            vmem((tracers, levels, merid), F32),
            vmem((tracers, levels), F32),
            vmem((levels, levels), F32),
            vmem((levels, 4 * levels), BF16),
            vmem((levels, merid), F32),
            pltpu.SMEM((1, tracers), F32),
            pltpu.SMEM((4,), jnp.int32),
            pltpu.SMEM((4,), jnp.int32),
            vmem((2, tracers, columns, merid), F32),
            vmem((2, tracers, columns, merid), F32),
            vmem((tracers, merid), F32),
            vmem((tracers, merid), F32),
            vmem((tracers, merid), F32),
            vmem((4, 8, merid), F32),
            vmem((2, tracers, columns, merid), F32),
            vmem((2, tracers, levels, merid), F32),
            vmem((tracers, levels, merid), BF16),
            vmem((tracers, levels, merid), BF16),
            vmem((tracers, levels, merid), F32),
            vmem((tracers + 1, levels, merid), BF16),
            vmem((tracers + 1, levels, merid), BF16),
            vmem((tracers, levels, merid), F32),
            vmem((levels, merid), F32),
        ]
        + [vmem((8, merid), F32)] * 5
        + [vmem((40, merid), F32)] * 3
        + [vmem((32, merid), F32)] * 5
        + [
            dma((columns + 1,)),
            dma((6,)),
            dma((15,)),
            dma((15,)),
            pltpu.SemaphoreType.REGULAR,
        ],
        compiler_params=pltpu.CompilerParams(
            collective_id=0, has_side_effects=True, vmem_limit_bytes=48 * 2**20
        ),
    )(
        *(pltpu.with_memory_space_constraint(v, pltpu.MemorySpace.HBM) for v in (
        local,
        rows,
        flow.reshape(2, levels, columns, merid),
        diffusion.reshape(tracers, levels),
        column_solve.reshape(levels, levels),
        exchange_rate,
        block_map,
        ice_mask,
    )))
    result = pl.pallas_call(
        finish_kernel,
        out_shape=jax.ShapeDtypeStruct((tracers, levels, columns, 1, merid), F32),
        in_specs=[pl.BlockSpec(memory_space=pltpu.VMEM)],
        out_specs=hbm,
        scratch_shapes=[dma((16,))],
        compiler_params=pltpu.CompilerParams(vmem_limit_bytes=48 * 2**20),
    )(result)
    return result.reshape(1, tracers, levels, columns, merid)


def solution(mesh):
    return jax.shard_map(
        on_device,
        mesh=mesh,
        in_specs=(
            P("fluid", None, None, "zon", "mer"),
            P("fluid", None, None, "zon", "mer"),
            P("fluid", None, None),
            P("fluid", None, None),
            P("fluid", None),
            P("mer"),
            P("mer"),
        ),
        out_specs=P("fluid", None, None, "zon", "mer"),
        check_vma=False,
    )
```

```python
import jax
import jax.numpy as jnp
from jax import lax
from jax.experimental import pallas as pl
from jax.experimental.pallas import tpu as pltpu
from jax.sharding import PartitionSpec as P

MESH = pl.DeviceIdType.MESH
F32 = jnp.float32
BF16 = jnp.bfloat16


def split(value):
    high = value.astype(BF16)
    low = (value - high.astype(F32)).astype(BF16)
    return high, low


def stacked(value):
    high, low = split(value)
    return jnp.concatenate([high, high, low, low], axis=0)


def window_kernel(
    state, rows, flow, diffusion, solve, rate, block_map, ice_mask,
    res,
    q0, q1, flow_v, flow_n, half_c, half_d, kappa, diff_v, solve_v, lhs, surf_col,
    rate_s, map_s, ice_s,
    own_surf, other_surf, own_late, other_late, west_surf, weights, increment,
    halo_e, west_out, west_in, west_row, ring_out, ring_in, wests, corner_shift,
    mini_out, mini_in, corner_out, corner_n, corner_s,
    pack_out, pack_n, pack_s, pack2_out, pack2_n, pack2_s, flow_p, kappa_p,
    load_sem, small_sem, send_sem, recv_sem, hello, token,
):
    fluid = lax.axis_index("fluid")
    zon = lax.axis_index("zon")
    mer = lax.axis_index("mer")
    zons = lax.axis_size("zon")
    mers = lax.axis_size("mer")
    levels, columns = 64, 16
    last = columns - 1
    east, west = lax.rem(zon + 1, zons), lax.rem(zon + zons - 1, zons)
    north, south = lax.rem(mer + 1, mers), lax.rem(mer + mers - 1, mers)
    across = 1 - fluid
    barrier = pltpu.get_barrier_semaphore()

    def greet(peers):
        for peer in peers:
            pl.semaphore_signal(barrier, inc=1, device_id=peer, device_id_type=MESH)

    before_seam = lax.rem(zon, 24) == 23
    after_seam = lax.rem(zon, 24) == 0
    greet(((fluid, west, mer), (fluid, west, north), (fluid, west, south), (across, west, mer)))

    @pl.when(jnp.logical_not(before_seam))
    def _():
        greet(((fluid, zon, north), (fluid, zon, south), (across, zon, mer)))

    surface = (levels - 1) * (1 - fluid)
    is_atm = fluid == 0

    loads = [pltpu.make_async_copy(rows.at[:, :, x, 0, :], q0.at[x + 1], load_sem.at[x]) for x in range(columns)]
    loads[last].start()
    flow_load = pltpu.make_async_copy(flow, flow_v, load_sem.at[columns])
    flow_load.start()
    smalls = [
        pltpu.make_async_copy(block_map, map_s, small_sem.at[0]),
        pltpu.make_async_copy(ice_mask, ice_s, small_sem.at[1]),
        pltpu.make_async_copy(rate, rate_s, small_sem.at[2]),
        pltpu.make_async_copy(solve, solve_v, small_sem.at[3]),
        pltpu.make_async_copy(diffusion, diff_v, small_sem.at[4]),
        pltpu.make_async_copy(state.at[:, surface], own_surf.at[0], small_sem.at[5]),
    ]
    for copy in smalls:
        copy.start()
    for x in (last - 1, *range(last - 1)):
        loads[x].start()

    def copy_to(slot, peer, source, target):
        return pltpu.make_async_remote_copy(
            src_ref=source,
            dst_ref=target,
            send_sem=send_sem.at[slot],
            recv_sem=recv_sem.at[slot],
            device_id=peer,
            device_id_type=MESH,
        )

    row_w = copy_to(0, (fluid, east, mer), west_out, west_in)
    surf_w = copy_to(1, (across, east, mer), rows.at[:, surface, last, 0, :], west_surf)
    surf_0 = copy_to(2, (across, zon, mer), state.at[:, surface], other_surf.at[0])
    corner_to_n = copy_to(3, (fluid, east, north), corner_out, corner_s)
    corner_to_s = copy_to(4, (fluid, east, south), corner_out, corner_n)
    ring = copy_to(5, (fluid, east, mer), ring_out, ring_in)
    mini_w = copy_to(6, (fluid, east, mer), mini_out, mini_in)
    pack_to_n = copy_to(7, (fluid, zon, north), pack_out, pack_s)
    pack_to_s = copy_to(8, (fluid, zon, south), pack_out, pack_n)
    row_e = copy_to(9, (fluid, west, mer), rows.at[:, :, 0, 0, :], halo_e.at[0])
    surf_1 = copy_to(10, (across, zon, mer), own_surf.at[1], other_surf.at[1])
    pack2_to_n = copy_to(11, (fluid, zon, north), pack2_out, pack2_s)
    pack2_to_s = copy_to(12, (fluid, zon, south), pack2_out, pack2_n)
    surf_late = copy_to(13, (across, zon, mer), own_late, other_late)
    row2_e = copy_to(14, (fluid, west, mer), q1.at[1], halo_e.at[1])

    def send(*copies):
        for copy in copies:
            copy.start()

    def send_before_seam(*copies):
        pl.when(before_seam)(lambda: send(*copies))

    @pl.when(before_seam)
    def _():
        pl.semaphore_wait(barrier, 4)
        for peer in ((fluid, east, mer), (fluid, east, north), (across, east, mer)):
            pl.semaphore_signal(hello, inc=1, device_id=peer, device_id_type=MESH)
        send(surf_w)

    lane = lax.broadcasted_iota(jnp.int32, (levels, 128), 1)
    lane32 = lax.broadcasted_iota(jnp.int32, (32, 128), 1)
    even = (lane32 & 1) == 0
    edge = (lane == 0) | (lane == 127)

    def packed_lanes(block, j, total):
        for half in range(2):
            start = 64 * half + 2 * j
            piece = block[32 * half : 32 * half + 32]
            total = jnp.where((lane32 >> 1) == (start >> 1), pltpu.roll(piece, (start + 1) % 128, 1), total)
        return total

    def pack(field):
        total = jnp.zeros((32, 128), F32)
        for x in range(columns):
            for t in range(2):
                total = packed_lanes(field[x + 1, t], 2 * x + t, total)
        return total

    lane8 = lax.broadcasted_iota(jnp.int32, (8, 128), 1)

    def mini(total):
        small = jnp.zeros((8, 128), F32)
        for i in range(4):
            piece = total[8 * i : 8 * i + 8]
            small = jnp.where(((lane8 >> 2) & 15) == 15 - i, pltpu.roll(piece, (128 - 4 * i) % 128, 1), small)
        return small

    def from_mini(small):
        return jnp.concatenate([small] + [pltpu.roll(small, 4 * i, 1) for i in range(1, 4)], axis=0)

    def unpacked(terms):
        return jnp.concatenate([terms, pltpu.roll(terms, 64, 1)], axis=0)

    def at_edges(sides, j):
        return pltpu.roll(sides, (127 - 2 * j) % 128, 1)

    loads[last].wait()
    west_out[...] = q0[columns].astype(BF16)
    total = jnp.zeros((32, 128), F32)
    for t in range(2):
        total = packed_lanes(q0[columns, t], 2 * last + t, total)
    corner_out[...] = mini(total)
    send_before_seam(corner_to_n, corner_to_s, row_w)

    for copy in smalls:
        copy.wait()
    eye = lax.broadcasted_iota(jnp.int32, (levels, levels), 0) == lax.broadcasted_iota(jnp.int32, (levels, levels), 1)
    for t in range(2):
        line = jnp.broadcast_to(diff_v[t : t + 1, :], (levels, levels))
        kappa[t] = jnp.broadcast_to(jnp.sum(jnp.where(eye, line, 0.0), axis=1, keepdims=True), (levels, 128))
    matrix = solve_v[...]
    twice = jnp.concatenate([matrix, matrix], axis=1)
    high = twice.astype(BF16).astype(F32)
    pair = jnp.where(lane < levels, high, twice - high)
    lhs[...] = jnp.concatenate([pair, pair], axis=1).astype(BF16)
    at_surface = lax.broadcasted_iota(jnp.int32, (levels, levels), 1) == surface
    surf_col[...] = jnp.broadcast_to(
        jnp.sum(jnp.where(at_surface, matrix, 0.0), axis=1, keepdims=True), (levels, 128)
    )
    quarter = (lane32 >> 1) & 1
    kappa_p[...] = jnp.where(
        quarter == 0,
        jnp.where(lane32 < 64, kappa[0, 0:32], kappa[0, 32:64]),
        jnp.where(lane32 < 64, kappa[1, 0:32], kappa[1, 32:64]),
    )
    zero_block = jnp.zeros((2, levels, 128), F32)
    for field in (q0, q1):
        field[0] = zero_block
        field[columns + 1] = zero_block

    def solve_of(value):
        return jnp.dot(lhs[...], stacked(value), preferred_element_type=F32)

    def interior(field, target, offset, x):
        c = half_c[x]
        d = half_d[x]
        parts = []
        for t in range(2):
            k = kappa[t]
            q = field[x + 1, t]
            parts.append(
                (1.0 - 4.0 * k) * q
                + (k - c) * field[x + 2, t]
                + (k + c) * field[x, t]
                + (k - d) * jnp.where(lane == 127, 0.0, pltpu.roll(q, 127, 1))
                + (k + d) * jnp.where(lane == 0, 0.0, pltpu.roll(q, 1, 1))
            )
        solved = solve_of(jnp.concatenate(parts, axis=1))
        target[x + offset, 0] = solved[:, :128]
        target[x + offset, 1] = solved[:, 128:]

    flow_load.wait()
    for piece in range(2):
        flow_n[piece] = flow_v[piece].astype(F32).reshape(levels * columns, 128) * 0.5

    def turn(x):
        half_c[x] = flow_n[0, pl.ds(x, levels, stride=columns), :]
        half_d[x] = flow_n[1, pl.ds(x, levels, stride=columns), :]

    turn(last)
    total = jnp.zeros((32, 128), F32)
    for t in range(2):
        total = packed_lanes(half_d[last], 2 * last + t, total)
    mini_out[...] = mini(total)
    loads[last - 1].wait()
    interior(q0, q1, 1, last)
    ring_out[0] = half_c[last].astype(BF16)
    ring_out[1:3] = q1[columns].astype(BF16)
    send_before_seam(ring, mini_w)

    for x in range(last):
        turn(x)
        for t in range(2):
            total = packed_lanes(half_d[x], 2 * x + t, total)
    flow_p[...] = total
    for x in range(last - 1):
        loads[x].wait()
    pack_out[0:32] = pack(q0)
    ends = jnp.zeros((32, 128), F32)
    for t in range(2):
        ends = packed_lanes(half_c[0], 2 * last + t, ends)
    pack_out[32:40] = mini(ends)

    @pl.when(jnp.logical_not(before_seam))
    def _():
        pl.semaphore_wait(barrier, 7)
        send(corner_to_n, corner_to_s, row_w, ring, mini_w, surf_w, surf_0, pack_to_n, pack_to_s)

    block_of = lax.broadcasted_iota(jnp.int32, (8, 128), 1) // 32
    base = 4 * mer
    for k in range(4):
        line = jnp.zeros((8, 128), F32)
        for o in range(4):
            b = (o + k) % 4
            ocean_hit = jnp.where(map_s[o] - base == b, 1 - ice_s[o], 0)
            atm_hit = jnp.where(map_s[b] - base == o, 1 - ice_s[b], 0)
            hit = jnp.where(is_atm, atm_hit, ocean_hit).astype(F32)
            line = jnp.where(block_of == o, hit, line)
        weights[k] = line

    def first_body(x, carry):
        interior(q0, q1, 1, x)
        return carry

    lax.fori_loop(0, last, first_body, 0, unroll=3)

    def exchange(own, other, repeat):
        shares = [jnp.concatenate([weights[k]] * repeat, axis=0) if repeat else weights[k][0:2] for k in range(4)]
        flux = -(shares[0] + shares[1] + shares[2] + shares[3]) * own
        for k in range(4):
            flux = flux + shares[k] * (other if k == 0 else pltpu.roll(other, 128 - 32 * k, 1))
        return flux

    def increments(step):
        for t in range(2):
            increment[step, t] = exchange(own_surf[step, t], other_surf[step, t], 2) * rate_s[0, t]

    has_north = jnp.where(mer == mers - 1, 0.0, 1.0)
    has_south = jnp.where(mer == 0, 0.0, 1.0)

    def near(from_n, from_s):
        return jnp.where(even, pltpu.roll(from_n, 127, 1) * has_north, pltpu.roll(from_s, 1, 1) * has_south)

    def side_terms(beyond, half):
        return (kappa_p[...] + jnp.where(even, -half, half)) * beyond

    @pl.when(jnp.logical_not(after_seam))
    def _():
        row_w.wait_recv()
        row_e.start()

    @pl.when(before_seam)
    def _():
        pl.semaphore_wait(token, 2)
        send(surf_0, pack_to_n, pack_to_s)

    surf_0.wait_recv()
    increments(0)
    pack_to_n.wait_recv()
    pack_to_s.wait_recv()
    sides = solve_of(unpacked(side_terms(near(pack_n[0:32], pack_s[0:32]), flow_p[...])))
    column = surf_col[...]

    def corrected(step, target, offset, x):
        return [
            target[x + offset, t]
            + column * increment[step, t, x : x + 1, :]
            + jnp.where(edge, at_edges(sides, 2 * x + t), 0.0)
            for t in range(2)
        ]

    def keep(x, values):
        for t in range(2):
            q1[x + 1, t] = values[t]
            own_surf[1, t, x : x + 1, :] = q1[x + 1, t, pl.ds(surface, 1), :]

    for x in range(last):
        keep(x, corrected(0, q1, 1, x))
    row_e.wait_recv()
    k_c = [kappa[t] - half_c[last] for t in range(2)]
    solved = solve_of(jnp.concatenate([k_c[t] * halo_e[0, t] for t in range(2)], axis=1))
    values = corrected(0, q1, 1, last)
    keep(last, [values[0] + solved[:, :128], values[1] + solved[:, 128:]])
    send(surf_1)
    pack2_out[...] = pack(q1)
    send(pack2_to_n, pack2_to_s)

    def west_side(late):
        if late:
            pl.semaphore_wait(hello, 3)
            for peer in ((fluid, west, mer), (fluid, west, south)):
                pl.semaphore_signal(token, inc=1, device_id=peer, device_id_type=MESH)
            row_e.start()
            row_w.wait_recv()
        west_row[...] = west_in[...].astype(F32)
        solved = solve_of(jnp.concatenate([(kappa[t] + half_c[0]) * west_row[t] for t in range(2)], axis=1))
        for t in range(2):
            q1[1, t] = q1[1, t] + solved[:, 128 * t : 128 * t + 128]
            own_late[t : t + 1, :] = q1[1, t, pl.ds(surface, 1), :]
        send(surf_late, row2_e)
        ring.wait_recv()
        k_w = [kappa[t] - ring_in[0].astype(F32) for t in range(2)]
        own = solve_of(jnp.concatenate([k_w[t] * q0[1, t] for t in range(2)], axis=1))
        surf_w.wait_recv()
        west_own = jnp.concatenate([west_row[t, pl.ds(surface, 1), :] for t in range(2)], axis=0)
        west_flux = exchange(west_own, west_surf[...], 0) * rates
        for t in range(2):
            wests[t] = (
                ring_in[1 + t].astype(F32) + own[:, 128 * t : 128 * t + 128] + column * west_flux[t : t + 1]
            )

    def west_corners():
        mini_w.wait_recv()
        corner_to_n.wait_recv()
        corner_to_s.wait_recv()
        from_n = from_mini(corner_n[...])
        from_s = from_mini(corner_s[...])
        corners = side_terms(near(from_n, from_s), from_mini(mini_in[...]))
        mixed = jnp.where(
            even,
            (kappa_p[...] + from_mini(pack_s[32:40])) * from_s * has_south,
            (kappa_p[...] + from_mini(pack_n[32:40])) * from_n * has_north,
        )
        solved = solve_of(jnp.concatenate([unpacked(corners), unpacked(mixed)], axis=1))
        for t in range(2):
            wests[t] = wests[t] + jnp.where(edge, at_edges(solved[:, 0:128], 2 * last + t), 0.0)
        mixed = solved[:, 128:256]
        corner_shift[...] = jnp.where((lane & 1) == 0, pltpu.roll(mixed, 67, 1), pltpu.roll(mixed, 69, 1))

    tracer = lax.broadcasted_iota(jnp.int32, (2, 128), 0)
    rates = jnp.where(tracer == 0, rate_s[0, 0], rate_s[0, 1])

    @pl.when(jnp.logical_not(after_seam))
    def _():
        west_side(False)
        west_corners()

    def second_body(x, carry):
        interior(q1, res, 0, x)
        return carry

    lax.fori_loop(2, columns, second_body, 0, unroll=2)
    pl.when(after_seam)(lambda: west_side(True))
    surf_1.wait_recv()
    increments(1)
    pack2_to_n.wait_recv()
    pack2_to_s.wait_recv()
    beyond = near(pack2_n[...], pack2_s[...])
    sides = solve_of(unpacked(side_terms(beyond, flow_p[...])))
    for x in range(2, columns):
        values = corrected(1, res, 0, x)
        for t in range(2):
            res[x, t] = values[t]
    beyond = unpacked(beyond)

    row2_e.wait_recv()
    solved = solve_of(
        jnp.concatenate([(kappa[t] - half_c[last]) * halo_e[1, t] for t in range(2)], axis=1)
    )
    for t in range(2):
        res[last, t] = res[last, t] + solved[:, 128 * t : 128 * t + 128]
    pl.when(after_seam)(west_corners)
    firsts = [q1[1, t] for t in range(2)]
    beyond_first = beyond + corner_shift[...]

    def full(k, c, d, q, to_east, to_west, around):
        return (
            (1.0 - 4.0 * k) * q
            + (k - c) * to_east
            + (k + c) * to_west
            + (k - d) * jnp.where(lane == 127, around, pltpu.roll(q, 127, 1))
            + (k + d) * jnp.where(lane == 0, around, pltpu.roll(q, 1, 1))
        )

    updates = [
        full(kappa[t], half_c[0], half_d[0], firsts[t], q1[2, t], wests[t], at_edges(beyond_first, t)) for t in range(2)
    ] + [
        full(kappa[t], half_c[1], half_d[1], q1[2, t], q1[3, t], firsts[t], at_edges(beyond, 2 + t)) for t in range(2)
    ]
    solved = solve_of(jnp.concatenate(updates, axis=1))
    for t in range(2):
        res[1, t] = solved[:, 256 + 128 * t : 384 + 128 * t] + column * increment[1, t, 1:2, :]
    surf_late.wait_recv()
    late_flux = exchange(own_late[...], other_late[...], 0) * rates
    for t in range(2):
        res[0, t] = solved[:, 128 * t : 128 * t + 128] + column * late_flux[t : t + 1]

    for copy in (
        row_w, surf_w, surf_0, corner_to_n, corner_to_s, ring, mini_w, pack_to_n,
        pack_to_s, row_e, surf_1, pack2_to_n, pack2_to_s, surf_late, row2_e,
    ):
        copy.wait_send()


def finish_kernel(source, out, sem):
    copies = [pltpu.make_async_copy(source.at[x], out.at[:, :, x, 0, :], sem.at[x]) for x in range(16)]
    for copy in copies:
        copy.start()
    for copy in copies:
        copy.wait()


def on_device(state, flow, diffusion, column_solve, exchange_rate, block_map, ice_mask):
    _, tracers, levels, columns, merid = state.shape
    local = state.reshape(tracers, levels, columns, merid)
    rows = state.reshape(tracers, levels, columns, 1, merid)
    vmem = pltpu.VMEM
    dma = pltpu.SemaphoreType.DMA
    hbm = pl.BlockSpec(memory_space=pltpu.MemorySpace.HBM)
    result = pl.pallas_call(
        window_kernel,
        out_shape=jax.ShapeDtypeStruct((columns, tracers, levels, merid), F32),
        in_specs=[hbm] * 8,
        out_specs=pl.BlockSpec(memory_space=pltpu.VMEM),
        scratch_shapes=[
            vmem((columns + 2, tracers, levels, merid), F32),
            vmem((columns + 2, tracers, levels, merid), F32),
            vmem((2, levels, columns, merid), BF16),
            vmem((2, levels * columns, merid), F32),
            vmem((columns, levels, merid), F32),
            vmem((columns, levels, merid), F32),
            vmem((tracers, levels, merid), F32),
            vmem((tracers, levels), F32),
            vmem((levels, levels), F32),
            vmem((levels, 4 * levels), BF16),
            vmem((levels, merid), F32),
            pltpu.SMEM((1, tracers), F32),
            pltpu.SMEM((4,), jnp.int32),
            pltpu.SMEM((4,), jnp.int32),
            vmem((2, tracers, columns, merid), F32),
            vmem((2, tracers, columns, merid), F32),
            vmem((tracers, merid), F32),
            vmem((tracers, merid), F32),
            vmem((tracers, merid), F32),
            vmem((4, 8, merid), F32),
            vmem((2, tracers, columns, merid), F32),
            vmem((2, tracers, levels, merid), F32),
            vmem((tracers, levels, merid), BF16),
            vmem((tracers, levels, merid), BF16),
            vmem((tracers, levels, merid), F32),
            vmem((tracers + 1, levels, merid), BF16),
            vmem((tracers + 1, levels, merid), BF16),
            vmem((tracers, levels, merid), F32),
            vmem((levels, merid), F32),
        ]
        + [vmem((8, merid), F32)] * 5
        + [vmem((40, merid), F32)] * 3
        + [vmem((32, merid), F32)] * 5
        + [
            dma((columns + 1,)),
            dma((6,)),
            dma((15,)),
            dma((15,)),
            pltpu.SemaphoreType.REGULAR,
            pltpu.SemaphoreType.REGULAR,
        ],
        compiler_params=pltpu.CompilerParams(
            collective_id=0, has_side_effects=True, vmem_limit_bytes=48 * 2**20
        ),
    )(
        *(pltpu.with_memory_space_constraint(v, pltpu.MemorySpace.HBM) for v in (
        local,
        rows,
        flow.reshape(2, levels, columns, merid),
        diffusion.reshape(tracers, levels),
        column_solve.reshape(levels, levels),
        exchange_rate,
        block_map,
        ice_mask,
    )))
    result = pl.pallas_call(
        finish_kernel,
        out_shape=jax.ShapeDtypeStruct((tracers, levels, columns, 1, merid), F32),
        in_specs=[pl.BlockSpec(memory_space=pltpu.VMEM)],
        out_specs=hbm,
        scratch_shapes=[dma((16,))],
        compiler_params=pltpu.CompilerParams(vmem_limit_bytes=48 * 2**20),
    )(result)
    return result.reshape(1, tracers, levels, columns, merid)


def solution(mesh):
    return jax.shard_map(
        on_device,
        mesh=mesh,
        in_specs=(
            P("fluid", None, None, "zon", "mer"),
            P("fluid", None, None, "zon", "mer"),
            P("fluid", None, None),
            P("fluid", None, None),
            P("fluid", None),
            P("mer"),
            P("mer"),
        ),
        out_specs=P("fluid", None, None, "zon", "mer"),
        check_vma=False,
    )
```

```python
import jax
import jax.numpy as jnp
from jax import lax
from jax.experimental import pallas as pl
from jax.experimental.pallas import tpu as pltpu
from jax.sharding import PartitionSpec as P

MESH = pl.DeviceIdType.MESH
F32 = jnp.float32
BF16 = jnp.bfloat16


def split(value):
    high = value.astype(BF16)
    low = (value - high.astype(F32)).astype(BF16)
    return high, low


def stacked(value):
    high, low = split(value)
    return jnp.concatenate([high, high, low, low], axis=0)


def window_kernel(
    state, rows, flow, diffusion, solve, rate, block_map, ice_mask,
    res,
    q0, q1, flow_v, flow_n, half_c, half_d, kappa, diff_v, solve_v, lhs, surf_col,
    rate_s, map_s, ice_s,
    own_surf, other_surf, own_late, other_late, west_surf, weights, increment,
    halo_e, west_out, west_in, west_row, ring_out, ring_in, wests, corner_shift,
    mini_out, mini_in, corner_out, corner_n, corner_s,
    pack_out, pack_n, pack_s, pack2_out, pack2_n, pack2_s, flow_p, kappa_p,
    load_sem, small_sem, send_sem, recv_sem, hello, token,
):
    fluid = lax.axis_index("fluid")
    zon = lax.axis_index("zon")
    mer = lax.axis_index("mer")
    zons = lax.axis_size("zon")
    mers = lax.axis_size("mer")
    levels, columns = 64, 16
    last = columns - 1
    east, west = lax.rem(zon + 1, zons), lax.rem(zon + zons - 1, zons)
    north, south = lax.rem(mer + 1, mers), lax.rem(mer + mers - 1, mers)
    across = 1 - fluid
    barrier = pltpu.get_barrier_semaphore()

    def greet(peers):
        for peer in peers:
            pl.semaphore_signal(barrier, inc=1, device_id=peer, device_id_type=MESH)

    before_seam = lax.rem(zon, 24) == 23
    after_seam = lax.rem(zon, 24) == 0
    greet(((fluid, west, mer), (fluid, west, north), (fluid, west, south), (across, west, mer)))

    @pl.when(jnp.logical_not(before_seam))
    def _():
        greet(((fluid, zon, north), (fluid, zon, south), (across, zon, mer)))

    surface = (levels - 1) * (1 - fluid)
    is_atm = fluid == 0

    loads = [pltpu.make_async_copy(rows.at[:, :, x, 0, :], q0.at[x + 1], load_sem.at[x]) for x in range(columns)]
    loads[last].start()
    flow_load = pltpu.make_async_copy(flow, flow_v, load_sem.at[columns])
    flow_load.start()
    smalls = [
        pltpu.make_async_copy(block_map, map_s, small_sem.at[0]),
        pltpu.make_async_copy(ice_mask, ice_s, small_sem.at[1]),
        pltpu.make_async_copy(rate, rate_s, small_sem.at[2]),
        pltpu.make_async_copy(solve, solve_v, small_sem.at[3]),
        pltpu.make_async_copy(diffusion, diff_v, small_sem.at[4]),
        pltpu.make_async_copy(state.at[:, surface], own_surf.at[0], small_sem.at[5]),
    ]
    for copy in smalls:
        copy.start()
    for x in (last - 1, *range(last - 1)):
        loads[x].start()

    def copy_to(slot, peer, source, target):
        return pltpu.make_async_remote_copy(
            src_ref=source,
            dst_ref=target,
            send_sem=send_sem.at[slot],
            recv_sem=recv_sem.at[slot],
            device_id=peer,
            device_id_type=MESH,
        )

    row_w = copy_to(0, (fluid, east, mer), west_out, west_in)
    surf_w = copy_to(1, (across, east, mer), rows.at[:, surface, last, 0, :], west_surf)
    surf_0 = copy_to(2, (across, zon, mer), state.at[:, surface], other_surf.at[0])
    corner_to_n = copy_to(3, (fluid, east, north), corner_out, corner_s)
    corner_to_s = copy_to(4, (fluid, east, south), corner_out, corner_n)
    ring = copy_to(5, (fluid, east, mer), ring_out, ring_in)
    mini_w = copy_to(6, (fluid, east, mer), mini_out, mini_in)
    pack_to_n = copy_to(7, (fluid, zon, north), pack_out, pack_s)
    pack_to_s = copy_to(8, (fluid, zon, south), pack_out, pack_n)
    row_e = copy_to(9, (fluid, west, mer), rows.at[:, :, 0, 0, :], halo_e.at[0])
    surf_1 = copy_to(10, (across, zon, mer), own_surf.at[1], other_surf.at[1])
    pack2_to_n = copy_to(11, (fluid, zon, north), pack2_out, pack2_s)
    pack2_to_s = copy_to(12, (fluid, zon, south), pack2_out, pack2_n)
    surf_late = copy_to(13, (across, zon, mer), own_late, other_late)
    row2_e = copy_to(14, (fluid, west, mer), q1.at[1], halo_e.at[1])

    def send(*copies):
        for copy in copies:
            copy.start()

    def send_before_seam(*copies):
        pl.when(before_seam)(lambda: send(*copies))

    @pl.when(before_seam)
    def _():
        pl.semaphore_wait(barrier, 4)
        for peer in ((fluid, east, mer), (fluid, east, north), (across, east, mer)):
            pl.semaphore_signal(hello, inc=1, device_id=peer, device_id_type=MESH)
        send(surf_w)

    lane = lax.broadcasted_iota(jnp.int32, (levels, 128), 1)
    lane32 = lax.broadcasted_iota(jnp.int32, (32, 128), 1)
    even = (lane32 & 1) == 0
    edge = (lane == 0) | (lane == 127)

    def packed_lanes(block, j, total):
        for half in range(2):
            start = 64 * half + 2 * j
            piece = block[32 * half : 32 * half + 32]
            total = jnp.where((lane32 >> 1) == (start >> 1), pltpu.roll(piece, (start + 1) % 128, 1), total)
        return total

    def pack(field):
        total = jnp.zeros((32, 128), F32)
        for x in range(columns):
            for t in range(2):
                total = packed_lanes(field[x + 1, t], 2 * x + t, total)
        return total

    lane8 = lax.broadcasted_iota(jnp.int32, (8, 128), 1)

    def mini(total):
        small = jnp.zeros((8, 128), F32)
        for i in range(4):
            piece = total[8 * i : 8 * i + 8]
            small = jnp.where(((lane8 >> 2) & 15) == 15 - i, pltpu.roll(piece, (128 - 4 * i) % 128, 1), small)
        return small

    def from_mini(small):
        return jnp.concatenate([small] + [pltpu.roll(small, 4 * i, 1) for i in range(1, 4)], axis=0)

    def unpacked(terms):
        return jnp.concatenate([terms, pltpu.roll(terms, 64, 1)], axis=0)

    def at_edges(sides, j):
        return pltpu.roll(sides, (127 - 2 * j) % 128, 1)

    loads[last].wait()
    west_out[...] = q0[columns].astype(BF16)
    send_before_seam(row_w)
    total = jnp.zeros((32, 128), F32)
    for t in range(2):
        total = packed_lanes(q0[columns, t], 2 * last + t, total)
    corner_out[...] = mini(total)
    send_before_seam(corner_to_n, corner_to_s)

    for copy in smalls:
        copy.wait()
    eye = lax.broadcasted_iota(jnp.int32, (levels, levels), 0) == lax.broadcasted_iota(jnp.int32, (levels, levels), 1)
    for t in range(2):
        line = jnp.broadcast_to(diff_v[t : t + 1, :], (levels, levels))
        kappa[t] = jnp.broadcast_to(jnp.sum(jnp.where(eye, line, 0.0), axis=1, keepdims=True), (levels, 128))
    matrix = solve_v[...]
    twice = jnp.concatenate([matrix, matrix], axis=1)
    high = twice.astype(BF16).astype(F32)
    pair = jnp.where(lane < levels, high, twice - high)
    lhs[...] = jnp.concatenate([pair, pair], axis=1).astype(BF16)
    at_surface = lax.broadcasted_iota(jnp.int32, (levels, levels), 1) == surface
    surf_col[...] = jnp.broadcast_to(
        jnp.sum(jnp.where(at_surface, matrix, 0.0), axis=1, keepdims=True), (levels, 128)
    )
    quarter = (lane32 >> 1) & 1
    kappa_p[...] = jnp.where(
        quarter == 0,
        jnp.where(lane32 < 64, kappa[0, 0:32], kappa[0, 32:64]),
        jnp.where(lane32 < 64, kappa[1, 0:32], kappa[1, 32:64]),
    )
    zero_block = jnp.zeros((2, levels, 128), F32)
    for field in (q0, q1):
        field[0] = zero_block
        field[columns + 1] = zero_block

    def solve_of(value):
        return jnp.dot(lhs[...], stacked(value), preferred_element_type=F32)

    def interior(field, target, offset, x):
        c = half_c[x]
        d = half_d[x]
        parts = []
        for t in range(2):
            k = kappa[t]
            q = field[x + 1, t]
            parts.append(
                (1.0 - 4.0 * k) * q
                + (k - c) * field[x + 2, t]
                + (k + c) * field[x, t]
                + (k - d) * jnp.where(lane == 127, 0.0, pltpu.roll(q, 127, 1))
                + (k + d) * jnp.where(lane == 0, 0.0, pltpu.roll(q, 1, 1))
            )
        solved = solve_of(jnp.concatenate(parts, axis=1))
        target[x + offset, 0] = solved[:, :128]
        target[x + offset, 1] = solved[:, 128:]

    flow_load.wait()
    for piece in range(2):
        flow_n[piece] = flow_v[piece].astype(F32).reshape(levels * columns, 128) * 0.5

    def turn(x):
        half_c[x] = flow_n[0, pl.ds(x, levels, stride=columns), :]
        half_d[x] = flow_n[1, pl.ds(x, levels, stride=columns), :]

    turn(last)
    total = jnp.zeros((32, 128), F32)
    for t in range(2):
        total = packed_lanes(half_d[last], 2 * last + t, total)
    mini_out[...] = mini(total)
    loads[last - 1].wait()
    interior(q0, q1, 1, last)
    ring_out[0] = half_c[last].astype(BF16)
    ring_out[1:3] = q1[columns].astype(BF16)
    send_before_seam(ring, mini_w)

    for x in range(last):
        turn(x)
        for t in range(2):
            total = packed_lanes(half_d[x], 2 * x + t, total)
    flow_p[...] = total
    for x in range(last - 1):
        loads[x].wait()
    pack_out[0:32] = pack(q0)
    ends = jnp.zeros((32, 128), F32)
    for t in range(2):
        ends = packed_lanes(half_c[0], 2 * last + t, ends)
    pack_out[32:40] = mini(ends)

    @pl.when(jnp.logical_not(before_seam))
    def _():
        pl.semaphore_wait(barrier, 7)
        send(corner_to_n, corner_to_s, row_w, ring, mini_w, surf_w, surf_0, pack_to_n, pack_to_s)

    block_of = lax.broadcasted_iota(jnp.int32, (8, 128), 1) // 32
    base = 4 * mer
    for k in range(4):
        line = jnp.zeros((8, 128), F32)
        for o in range(4):
            b = (o + k) % 4
            ocean_hit = jnp.where(map_s[o] - base == b, 1 - ice_s[o], 0)
            atm_hit = jnp.where(map_s[b] - base == o, 1 - ice_s[b], 0)
            hit = jnp.where(is_atm, atm_hit, ocean_hit).astype(F32)
            line = jnp.where(block_of == o, hit, line)
        weights[k] = line

    def first_body(x, carry):
        interior(q0, q1, 1, x)
        return carry

    lax.fori_loop(0, last, first_body, 0, unroll=3)

    def exchange(own, other, repeat):
        shares = [jnp.concatenate([weights[k]] * repeat, axis=0) if repeat else weights[k][0:2] for k in range(4)]
        flux = -(shares[0] + shares[1] + shares[2] + shares[3]) * own
        for k in range(4):
            flux = flux + shares[k] * (other if k == 0 else pltpu.roll(other, 128 - 32 * k, 1))
        return flux

    def increments(step):
        for t in range(2):
            increment[step, t] = exchange(own_surf[step, t], other_surf[step, t], 2) * rate_s[0, t]

    has_north = jnp.where(mer == mers - 1, 0.0, 1.0)
    has_south = jnp.where(mer == 0, 0.0, 1.0)

    def near(from_n, from_s):
        return jnp.where(even, pltpu.roll(from_n, 127, 1) * has_north, pltpu.roll(from_s, 1, 1) * has_south)

    def side_terms(beyond, half):
        return (kappa_p[...] + jnp.where(even, -half, half)) * beyond

    @pl.when(jnp.logical_not(after_seam))
    def _():
        row_w.wait_recv()
        row_e.start()

    @pl.when(before_seam)
    def _():
        pl.semaphore_wait(token, 2)
        send(surf_0, pack_to_n, pack_to_s)

    surf_0.wait_recv()
    increments(0)
    pack_to_n.wait_recv()
    pack_to_s.wait_recv()
    sides = solve_of(unpacked(side_terms(near(pack_n[0:32], pack_s[0:32]), flow_p[...])))
    column = surf_col[...]

    def corrected(step, target, offset, x):
        return [
            target[x + offset, t]
            + column * increment[step, t, x : x + 1, :]
            + jnp.where(edge, at_edges(sides, 2 * x + t), 0.0)
            for t in range(2)
        ]

    def keep(x, values):
        for t in range(2):
            q1[x + 1, t] = values[t]
            own_surf[1, t, x : x + 1, :] = q1[x + 1, t, pl.ds(surface, 1), :]

    for x in range(last):
        keep(x, corrected(0, q1, 1, x))
    row_e.wait_recv()
    k_c = [kappa[t] - half_c[last] for t in range(2)]
    solved = solve_of(jnp.concatenate([k_c[t] * halo_e[0, t] for t in range(2)], axis=1))
    values = corrected(0, q1, 1, last)
    keep(last, [values[0] + solved[:, :128], values[1] + solved[:, 128:]])
    send(surf_1)
    pack2_out[...] = pack(q1)
    send(pack2_to_n, pack2_to_s)

    def west_side(late):
        if late:
            pl.semaphore_wait(hello, 3)
            for peer in ((fluid, west, mer), (fluid, west, south)):
                pl.semaphore_signal(token, inc=1, device_id=peer, device_id_type=MESH)
            row_e.start()
            row_w.wait_recv()
        west_row[...] = west_in[...].astype(F32)
        solved = solve_of(jnp.concatenate([(kappa[t] + half_c[0]) * west_row[t] for t in range(2)], axis=1))
        for t in range(2):
            q1[1, t] = q1[1, t] + solved[:, 128 * t : 128 * t + 128]
            own_late[t : t + 1, :] = q1[1, t, pl.ds(surface, 1), :]
        send(surf_late, row2_e)
        ring.wait_recv()
        k_w = [kappa[t] - ring_in[0].astype(F32) for t in range(2)]
        own = solve_of(jnp.concatenate([k_w[t] * q0[1, t] for t in range(2)], axis=1))
        surf_w.wait_recv()
        west_own = jnp.concatenate([west_row[t, pl.ds(surface, 1), :] for t in range(2)], axis=0)
        west_flux = exchange(west_own, west_surf[...], 0) * rates
        for t in range(2):
            wests[t] = (
                ring_in[1 + t].astype(F32) + own[:, 128 * t : 128 * t + 128] + column * west_flux[t : t + 1]
            )

    def west_corners():
        mini_w.wait_recv()
        corner_to_n.wait_recv()
        corner_to_s.wait_recv()
        from_n = from_mini(corner_n[...])
        from_s = from_mini(corner_s[...])
        corners = side_terms(near(from_n, from_s), from_mini(mini_in[...]))
        mixed = jnp.where(
            even,
            (kappa_p[...] + from_mini(pack_s[32:40])) * from_s * has_south,
            (kappa_p[...] + from_mini(pack_n[32:40])) * from_n * has_north,
        )
        solved = solve_of(jnp.concatenate([unpacked(corners), unpacked(mixed)], axis=1))
        for t in range(2):
            wests[t] = wests[t] + jnp.where(edge, at_edges(solved[:, 0:128], 2 * last + t), 0.0)
        mixed = solved[:, 128:256]
        corner_shift[...] = jnp.where((lane & 1) == 0, pltpu.roll(mixed, 67, 1), pltpu.roll(mixed, 69, 1))

    tracer = lax.broadcasted_iota(jnp.int32, (2, 128), 0)
    rates = jnp.where(tracer == 0, rate_s[0, 0], rate_s[0, 1])

    @pl.when(jnp.logical_not(after_seam))
    def _():
        west_side(False)
        west_corners()

    def second_body(x, carry):
        interior(q1, res, 0, x)
        return carry

    lax.fori_loop(2, columns, second_body, 0, unroll=2)
    pl.when(after_seam)(lambda: west_side(True))
    surf_1.wait_recv()
    increments(1)
    pack2_to_n.wait_recv()
    pack2_to_s.wait_recv()
    beyond = near(pack2_n[...], pack2_s[...])
    sides = solve_of(unpacked(side_terms(beyond, flow_p[...])))
    for x in range(2, columns):
        values = corrected(1, res, 0, x)
        for t in range(2):
            res[x, t] = values[t]
    beyond = unpacked(beyond)

    row2_e.wait_recv()
    solved = solve_of(
        jnp.concatenate([(kappa[t] - half_c[last]) * halo_e[1, t] for t in range(2)], axis=1)
    )
    for t in range(2):
        res[last, t] = res[last, t] + solved[:, 128 * t : 128 * t + 128]
    pl.when(after_seam)(west_corners)
    firsts = [q1[1, t] for t in range(2)]
    beyond_first = beyond + corner_shift[...]

    def full(k, c, d, q, to_east, to_west, around):
        return (
            (1.0 - 4.0 * k) * q
            + (k - c) * to_east
            + (k + c) * to_west
            + (k - d) * jnp.where(lane == 127, around, pltpu.roll(q, 127, 1))
            + (k + d) * jnp.where(lane == 0, around, pltpu.roll(q, 1, 1))
        )

    updates = [
        full(kappa[t], half_c[0], half_d[0], firsts[t], q1[2, t], wests[t], at_edges(beyond_first, t)) for t in range(2)
    ] + [
        full(kappa[t], half_c[1], half_d[1], q1[2, t], q1[3, t], firsts[t], at_edges(beyond, 2 + t)) for t in range(2)
    ]
    solved = solve_of(jnp.concatenate(updates, axis=1))
    for t in range(2):
        res[1, t] = solved[:, 256 + 128 * t : 384 + 128 * t] + column * increment[1, t, 1:2, :]
    surf_late.wait_recv()
    late_flux = exchange(own_late[...], other_late[...], 0) * rates
    for t in range(2):
        res[0, t] = solved[:, 128 * t : 128 * t + 128] + column * late_flux[t : t + 1]

    for copy in (
        row_w, surf_w, surf_0, corner_to_n, corner_to_s, ring, mini_w, pack_to_n,
        pack_to_s, row_e, surf_1, pack2_to_n, pack2_to_s, surf_late, row2_e,
    ):
        copy.wait_send()


def finish_kernel(source, out, sem):
    copies = [pltpu.make_async_copy(source.at[x], out.at[:, :, x, 0, :], sem.at[x]) for x in range(16)]
    for copy in copies:
        copy.start()
    for copy in copies:
        copy.wait()


def on_device(state, flow, diffusion, column_solve, exchange_rate, block_map, ice_mask):
    _, tracers, levels, columns, merid = state.shape
    local = state.reshape(tracers, levels, columns, merid)
    rows = state.reshape(tracers, levels, columns, 1, merid)
    vmem = pltpu.VMEM
    dma = pltpu.SemaphoreType.DMA
    hbm = pl.BlockSpec(memory_space=pltpu.MemorySpace.HBM)
    result = pl.pallas_call(
        window_kernel,
        out_shape=jax.ShapeDtypeStruct((columns, tracers, levels, merid), F32),
        in_specs=[hbm] * 8,
        out_specs=pl.BlockSpec(memory_space=pltpu.VMEM),
        scratch_shapes=[
            vmem((columns + 2, tracers, levels, merid), F32),
            vmem((columns + 2, tracers, levels, merid), F32),
            vmem((2, levels, columns, merid), BF16),
            vmem((2, levels * columns, merid), F32),
            vmem((columns, levels, merid), F32),
            vmem((columns, levels, merid), F32),
            vmem((tracers, levels, merid), F32),
            vmem((tracers, levels), F32),
            vmem((levels, levels), F32),
            vmem((levels, 4 * levels), BF16),
            vmem((levels, merid), F32),
            pltpu.SMEM((1, tracers), F32),
            pltpu.SMEM((4,), jnp.int32),
            pltpu.SMEM((4,), jnp.int32),
            vmem((2, tracers, columns, merid), F32),
            vmem((2, tracers, columns, merid), F32),
            vmem((tracers, merid), F32),
            vmem((tracers, merid), F32),
            vmem((tracers, merid), F32),
            vmem((4, 8, merid), F32),
            vmem((2, tracers, columns, merid), F32),
            vmem((2, tracers, levels, merid), F32),
            vmem((tracers, levels, merid), BF16),
            vmem((tracers, levels, merid), BF16),
            vmem((tracers, levels, merid), F32),
            vmem((tracers + 1, levels, merid), BF16),
            vmem((tracers + 1, levels, merid), BF16),
            vmem((tracers, levels, merid), F32),
            vmem((levels, merid), F32),
        ]
        + [vmem((8, merid), F32)] * 5
        + [vmem((40, merid), F32)] * 3
        + [vmem((32, merid), F32)] * 5
        + [
            dma((columns + 1,)),
            dma((6,)),
            dma((15,)),
            dma((15,)),
            pltpu.SemaphoreType.REGULAR,
            pltpu.SemaphoreType.REGULAR,
        ],
        compiler_params=pltpu.CompilerParams(
            collective_id=0, has_side_effects=True, vmem_limit_bytes=48 * 2**20
        ),
    )(
        *(pltpu.with_memory_space_constraint(v, pltpu.MemorySpace.HBM) for v in (
        local,
        rows,
        flow.reshape(2, levels, columns, merid),
        diffusion.reshape(tracers, levels),
        column_solve.reshape(levels, levels),
        exchange_rate,
        block_map,
        ice_mask,
    )))
    result = pl.pallas_call(
        finish_kernel,
        out_shape=jax.ShapeDtypeStruct((tracers, levels, columns, 1, merid), F32),
        in_specs=[pl.BlockSpec(memory_space=pltpu.VMEM)],
        out_specs=hbm,
        scratch_shapes=[dma((16,))],
        compiler_params=pltpu.CompilerParams(vmem_limit_bytes=48 * 2**20),
    )(result)
    return result.reshape(1, tracers, levels, columns, merid)


def solution(mesh):
    return jax.shard_map(
        on_device,
        mesh=mesh,
        in_specs=(
            P("fluid", None, None, "zon", "mer"),
            P("fluid", None, None, "zon", "mer"),
            P("fluid", None, None),
            P("fluid", None, None),
            P("fluid", None),
            P("mer"),
            P("mer"),
        ),
        out_specs=P("fluid", None, None, "zon", "mer"),
        check_vma=False,
    )
```
